32 devices in a mesh: seg: 2 (over x), genome: 16 (over z, y, core).
Axes of the slice: x: 2, y: 2, z: 4, core: 2. Of those that a mesh axis runs over, the one named last changes fastest.
Arguments:
- z_typed: float32 [256, 16384], P(None, ('seg', 'genome')), parts along dimension 1, may hold values from -8 to 8
- diag_inverse: float32 [32, 512, 512], P(('seg', 'genome')), parts along dimension 0
- coupling: float32 [32, 512, 256], P(('seg', 'genome')), parts along dimension 0
- impute_coef: bfloat16 [16384, 1024], P(('seg', 'genome')), parts along dimension 0, may hold values from -0.25 to 0.25
- anchor: int32 [16384], P(('seg', 'genome')), parts along dimension 0, may hold values from 0 to 8191, as said below
Outputs:
- imputed: float32 [256, 16384], P(None, ('seg', 'genome')), parts along dimension 1
The draws below stay inside these ranges and needn't reach their ends.
There are 2 independent parts, one for each index of `seg`. The reference program is written for one: setup_inputs(seed, part) draws one part's arguments, and reference() takes and returns one part's arrays. A program takes and returns all parts, laid end to end along the dimension named above; each array names one. Nothing has to cross between parts.
Inputs may be any that keep to these rules, and one draw needn't show every extreme that they name: The anchor of the untyped variant t lies in typed block t // 512, i.e. in columns (t // 512) * 512 to (t // 512 + 1) * 512 - 1.
All inputs are finite; a program needn't handle non-finite values.
Results may differ from the reference program's by a relative error of at most 0.002.
The reference program's roundings to bfloat16 on the way (of `alpha`) count: a program that leaves them out, or rounds other values in their place, can miss the bound.
Values may be sent and summed in bfloat16 or wider, within the bound.
A program may use at most 192 MiB of HBM per device.

```python
import jax
import jax.numpy as jnp
from jax import lax

TRAITS = 256
TYP_DEV = 512
HALF = 256
UNT_DEV = 512
BLOCKS = 16
TYPED = 8192
UNTYPED = 8192


def draw_diag_inverse(key, part):
    first, second = jax.random.split(key)
    noise = jax.random.normal(first, (BLOCKS, TYP_DEV, TYP_DEV), jnp.float32)
    lower_part = jnp.tril(noise, -1) * (0.3 / TYP_DEV ** 0.5)
    diag_values = jax.random.uniform(second, (BLOCKS, TYP_DEV), jnp.float32, 0.9, 1.1)
    rows_idx = jnp.arange(TYP_DEV)[:, None]
    cols_idx = jnp.arange(TYP_DEV)[None, :]
    on_diag = (rows_idx == cols_idx).astype(jnp.float32)
    return 0.25 * (lower_part + on_diag[None, :, :] * diag_values[:, :, None])


def block_order(one_key):
    return jax.random.permutation(one_key, HALF)


def draw_coupling(key, part):
    first, second, third, fourth = jax.random.split(key, 4)
    block_keys = jax.random.split(first, BLOCKS)
    orders = jax.vmap(block_order)(block_keys).astype(jnp.int32)
    signs = jax.random.randint(second, (BLOCKS, HALF), 0, 2).astype(jnp.float32) * 2.0 - 1.0
    columns = jnp.arange(HALF, dtype=jnp.int32)
    placed = (orders[:, :, None] == columns[None, None, :]).astype(jnp.float32) * signs[:, :, None]
    bottom_noise = jax.random.normal(third, (BLOCKS, HALF, HALF), jnp.float32)
    top_noise = jax.random.normal(fourth, (BLOCKS, TYP_DEV - HALF, HALF), jnp.float32)
    bottom = placed + bottom_noise * (0.05 / HALF ** 0.5)
    top = top_noise * (0.1 / TYP_DEV ** 0.5)
    factor = 0.5 ** (1.0 / BLOCKS) * 0.976 / 0.25
    return jnp.concatenate([top, bottom], axis=1) * factor


def draw_anchor(key, part):
    offsets = jax.random.randint(key, (UNTYPED,), 0, TYP_DEV)
    owners = jnp.arange(UNTYPED, dtype=jnp.int32) // UNT_DEV
    anchors = owners * TYP_DEV + offsets
    anchors = anchors.at[0].set(0)
    anchors = anchors.at[UNTYPED - 1].set(TYPED - 1)
    return anchors.astype(jnp.int32)


def level_of(stream_key, dims, cuts, smallest, top_value):
    def one(dim, blocks):
        heights = jax.random.uniform(jax.random.fold_in(jax.random.fold_in(stream_key, 6), dim), (blocks,), jnp.float32, smallest / len(cuts), top_value / len(cuts))
        return jnp.repeat(jnp.exp(heights), dims[dim] // blocks).reshape((-1,) + (1,) * (len(dims) - dim - 1))

    loudness = one(*cuts[0])
    for cut in cuts[1:]:
        loudness = loudness * one(*cut)
    return loudness


def bell_draw(rng, shape, width, limit, pieces=(), kind=jnp.bfloat16):
    drawn = width * jax.random.normal(rng, shape, jnp.float32)
    if pieces:
        drawn = drawn * level_of(rng, shape, pieces, -0.22, 0.18)
    return jnp.clip(drawn, -limit, limit).astype(kind)


def setup_inputs(seed: int = 0, part: int = 0) -> dict:
    splits = jax.random.split(jax.random.key(seed), 6)
    part_splits = jax.random.split(jax.random.fold_in(splits[5], part), 6)
    return {
        "z_typed": bell_draw(part_splits[0], (TRAITS, TYPED), 1.0, 8.0, ((1, 16),), jnp.float32),
        "diag_inverse": draw_diag_inverse(jax.random.fold_in(jax.random.fold_in(splits[5], part), 71), part),
        "coupling": draw_coupling(jax.random.fold_in(jax.random.fold_in(splits[5], part), 71), part),
        "impute_coef": bell_draw(part_splits[3], (UNTYPED, TYP_DEV + 2 * HALF), (2 * HALF) ** -0.5, 0.25, ((0, 16),)),
        "anchor": draw_anchor(jax.random.fold_in(jax.random.fold_in(splits[5], part), 71), part),
    }


precise = lax.Precision.HIGHEST


def reference(z_typed, diag_inverse, coupling, impute_coef, anchor):
    z_blocks = z_typed.reshape(TRAITS, BLOCKS, TYP_DEV).transpose(1, 0, 2)

    def forward_step(tail_in, inputs):
        z_block, inverse_block, couple = inputs
        projected = jnp.dot(inverse_block, couple, precision=precise)
        rows_now = jnp.dot(z_block, inverse_block.T, precision=precise) - jnp.dot(tail_in, projected.T, precision=precise)
        return rows_now[:, TYP_DEV - HALF:], rows_now

    start_tail = jnp.zeros((TRAITS, HALF), jnp.float32)
    _, all_rows = lax.scan(forward_step, start_tail, (z_blocks, diag_inverse, coupling))

    def backward_step(upper_in, inputs):
        rows_now, inverse_block, couple = inputs
        padded = jnp.concatenate([jnp.zeros((TRAITS, TYP_DEV - HALF), jnp.float32), upper_in], axis=1)
        solved = jnp.dot(rows_now - padded, inverse_block, precision=precise)
        return jnp.dot(solved, couple, precision=precise), solved

    _, all_alpha = lax.scan(backward_step, start_tail, (all_rows, diag_inverse, coupling), reverse=True)
    alpha = all_alpha.transpose(1, 0, 2).reshape(TRAITS, TYPED).astype(jnp.bfloat16)
    alpha_pad = jnp.concatenate([jnp.zeros((TRAITS, HALF), jnp.bfloat16), alpha, jnp.zeros((TRAITS, HALF), jnp.bfloat16)], axis=1)
    span = TYP_DEV + 2 * HALF
    coef_blocks = impute_coef.reshape(BLOCKS, UNT_DEV, span)
    anchor_blocks = anchor.reshape(BLOCKS, UNT_DEV)

    def impute_block(inputs):
        index, coef_block, anchor_block = inputs
        start = (index * TYP_DEV).astype(jnp.int32)
        window = lax.dynamic_slice_in_dim(alpha_pad, start, span, 1)
        columns = start - HALF + jnp.arange(span, dtype=jnp.int32)
        within = jnp.abs(columns[None, :] - anchor_block[:, None]) <= HALF
        masked = jnp.where(within, coef_block, jnp.zeros_like(coef_block))
        return lax.dot_general(window, masked, (((1,), (1,)), ((), ())), preferred_element_type=jnp.float32)

    parts = lax.map(impute_block, (jnp.arange(BLOCKS, dtype=jnp.int32), coef_blocks, anchor_blocks))
    return parts.transpose(1, 0, 2).reshape(TRAITS, UNTYPED)
```

```python
import functools

import jax
import jax.numpy as jnp
from jax import lax
from jax.experimental import pallas as pl
from jax.experimental.pallas import tpu as pltpu
from jax.sharding import PartitionSpec as P

F32 = jnp.float32
BF16 = jnp.bfloat16
NN = (((1,), (0,)), ((), ()))
NT = (((1,), (1,)), ((), ()))


def halves(x):
    high = x.astype(BF16)
    return high, (x - high.astype(F32)).astype(BF16)


def product(a, b, dims):
    return lax.dot_general(a, b, dims, preferred_element_type=F32)


def dot3(a, b, dims):
    return product(a[0], b[0], dims) + (product(a[0], b[1], dims) + product(a[1], b[0], dims))


def stacked(b):
    return jnp.concatenate([b[0], b[0], b[1]], axis=0)


def dot_stacked(x, weights):
    high, low = halves(x)
    return product(jnp.concatenate([high, low, high], axis=1), weights, NN)


def kernel(
    n, z_ref, inverse_ref, couple_ref, coef_ref, anchor_ref, out_ref,
    tail_in, tail_out, upper_in, upper_out, left_in, right_in, left_out, right_out,
    top_rows, forward_w, backward_w, inv_hi, inv_lo, proj_hi, proj_lo, masked,
    fs, fr, bs, br, es, er,
):
    me = lax.axis_index("genome")
    first, last = me == 0, me == n - 1
    right, left = lax.rem(me + 1, n), lax.rem(me + n - 1, n)
    chunks, rows, half = tail_in.shape
    typed = inverse_ref.shape[0]
    top = typed - half
    traits = chunks * rows

    barrier = pltpu.get_barrier_semaphore()
    for other in (left, right):
        pl.semaphore_signal(barrier, inc=1, device_id={"genome": other},
                            device_id_type=pl.DeviceIdType.MESH)

    def remote(src, dst, send, recv, other):
        return pltpu.make_async_remote_copy(
            src_ref=src, dst_ref=dst, send_sem=send, recv_sem=recv,
            device_id={"genome": other}, device_id_type=pl.DeviceIdType.MESH)

    def forward_copy(c):
        return remote(tail_out.at[c], tail_in.at[c], fs.at[c], fr.at[c], right)

    def backward_copy(c):
        return remote(upper_out.at[c], upper_in.at[c], bs.at[c], br.at[c], left)

    def to_right():
        return remote(left_out, left_in, es.at[0], er.at[0], right)

    def to_left():
        return remote(right_out, right_in, es.at[1], er.at[1], left)

    hi, lo = halves(inverse_ref[...])
    inv_hi[...] = hi
    inv_lo[...] = lo
    z_halves = halves(z_ref[...])
    solved_tail = dot3(z_halves, (inv_hi[pl.ds(top, half), :], inv_lo[pl.ds(top, half), :]), NT)
    tail_out[...] = solved_tail.reshape(chunks, rows, half)
    pl.semaphore_wait(barrier, 2)

    @pl.when(first)
    def _():
        def go(c, _):
            forward_copy(c).start()
            return 0
        lax.fori_loop(0, chunks, go, 0)
        tail_in[...] = jnp.zeros_like(tail_in)
        left_in[...] = jnp.zeros_like(left_in)

    @pl.when(last)
    def _():
        upper_in[...] = jnp.zeros_like(upper_in)
        right_in[...] = jnp.zeros_like(right_in)

    projected = dot3((inv_hi[...], inv_lo[...]), halves(couple_ref[...]), NN)
    hi, lo = halves(projected)
    proj_hi[...] = hi
    proj_lo[...] = lo
    chain = -projected[top:, :]
    forward_w[...] = stacked(halves(chain.T))
    backward_w[...] = stacked(halves(chain))
    solved_top = dot3(z_halves, (inv_hi[pl.ds(0, top), :], inv_lo[pl.ds(0, top), :]), NT)
    top_rows[...] = solved_top.reshape(chunks, rows, top)

    def make_mask():
        spread = 128
        units = anchor_ref.shape[1]
        nearest = jnp.broadcast_to(anchor_ref[...], (spread, units)).T
        start = me * typed - half
        lanes = lax.broadcasted_iota(jnp.int32, (units, spread), 1)
        for j in range(0, typed + 2 * half, spread):
            within = jnp.abs(lanes + (start + j) - nearest) <= half
            coef = coef_ref[:, j:j + spread].astype(F32)
            masked[:, j:j + spread] = jnp.where(within, coef, 0.0).astype(BF16)

    @pl.when(me >= n // 2)
    def _():
        make_mask()

    def source(tail, above, below):
        above = above - dot3(halves(tail), (proj_hi[pl.ds(0, top), :], proj_lo[pl.ds(0, top), :]), NT)
        all_rows = jnp.concatenate([above, below], axis=1)
        return above, dot3(halves(all_rows), (proj_hi[...], proj_lo[...]), NN)

    @pl.when(jnp.logical_not(first))
    def _():
        def step(c, _):
            forward_copy(c).wait_recv()
            tail_out[c] = tail_out[c] + dot_stacked(tail_in[c], forward_w[...])

            @pl.when(jnp.logical_not(last))
            def _():
                forward_copy(c).start()

            @pl.when(last)
            def _():
                above, add = source(tail_in[c], top_rows[c], tail_out[c])
                top_rows[c] = above
                upper_out[c] = add
                backward_copy(c).start()
            return 0
        lax.fori_loop(0, chunks, step, 0)

    @pl.when(jnp.logical_not(last))
    def _():
        above, add = source(tail_in[...].reshape(traits, half), top_rows[...].reshape(traits, top),
                            tail_out[...].reshape(traits, half))
        top_rows[...] = above.reshape(chunks, rows, top)
        upper_out[...] = add.reshape(chunks, rows, half)

    @pl.when(me < n // 2)
    def _():
        make_mask()

    @pl.when(jnp.logical_not(last))
    def _():
        def step(c, _):
            backward_copy(c).wait_recv()

            @pl.when(jnp.logical_not(first))
            def _():
                upper_out[c] = upper_out[c] + dot_stacked(upper_in[c], backward_w[...])
                backward_copy(c).start()
            return 0
        lax.fori_loop(0, chunks, step, 0)

    below = (tail_out[...] - upper_in[...]).reshape(traits, half)
    rows_now = jnp.concatenate([top_rows[...].reshape(traits, top), below], axis=1)
    weights = dot3(halves(rows_now), (inv_hi[...], inv_lo[...]), NN).astype(BF16)
    left_out[...] = weights[:, top:]
    right_out[...] = weights[:, :half]

    @pl.when(jnp.logical_not(last))
    def _():
        to_right().start()

    @pl.when(jnp.logical_not(first))
    def _():
        to_left().start()

    out_ref[...] = product(weights, masked[:, half:half + typed], NT)

    @pl.when(jnp.logical_not(last))
    def _():
        to_left().wait_recv()

    out_ref[...] += product(right_in[...], masked[:, half + typed:], NT)

    @pl.when(jnp.logical_not(first))
    def _():
        to_right().wait_recv()

    out_ref[...] += product(left_in[...], masked[:, :half], NT)

    @pl.when(jnp.logical_not(last))
    def _():
        def done(c, _):
            forward_copy(c).wait_send()
            return 0
        lax.fori_loop(0, chunks, done, 0)
        to_right().wait_send()

    @pl.when(jnp.logical_not(first))
    def _():
        def done(c, _):
            backward_copy(c).wait_send()
            return 0
        lax.fori_loop(0, chunks, done, 0)
        to_left().wait_send()


def per_device(n, z_typed, diag_inverse, coupling, impute_coef, anchor):
    traits, typed = z_typed.shape
    half = coupling.shape[2]
    units, span = impute_coef.shape
    top = typed - half
    chunks = next(k for k in (8, 4, 2, 1) if traits % (16 * k) == 0 or k == 1)
    rows = traits // chunks
    state = pltpu.VMEM((chunks, rows, half), F32)
    edge = pltpu.VMEM((traits, half), BF16)
    sems = pltpu.SemaphoreType.DMA((chunks,))
    return pl.pallas_call(
        functools.partial(kernel, n),
        out_shape=jax.ShapeDtypeStruct((traits, units), F32),
        in_specs=[pl.BlockSpec(memory_space=pltpu.VMEM)] * 5,
        out_specs=pl.BlockSpec(memory_space=pltpu.VMEM),
        scratch_shapes=[
            state, state, state, state, edge, edge, edge, edge,
            pltpu.VMEM((chunks, rows, top), F32),
            pltpu.VMEM((3 * half, half), BF16), pltpu.VMEM((3 * half, half), BF16),
            pltpu.VMEM((typed, typed), BF16), pltpu.VMEM((typed, typed), BF16),
            pltpu.VMEM((typed, half), BF16), pltpu.VMEM((typed, half), BF16),
            pltpu.VMEM((units, span), BF16),
            sems, sems, sems, sems,
            pltpu.SemaphoreType.DMA((2,)), pltpu.SemaphoreType.DMA((2,)),
        ],
        compiler_params=pltpu.CompilerParams(
            collective_id=0, has_side_effects=True, vmem_limit_bytes=48 * 1024 * 1024),
    )(z_typed, diag_inverse[0], coupling[0], impute_coef, anchor.reshape(1, units))


def solution(mesh):
    shared = ("seg", "genome")
    in_specs = (P(None, shared), P(shared, None, None), P(shared, None, None),
                P(shared, None), P(shared))
    return jax.shard_map(
        functools.partial(per_device, mesh.shape["genome"]), mesh=mesh, in_specs=in_specs,
        out_specs=P(None, shared), check_vma=False)
```

```python
import functools

import jax
import jax.numpy as jnp
from jax import lax
from jax.experimental import pallas as pl
from jax.experimental.pallas import tpu as pltpu
from jax.sharding import PartitionSpec as P

F32 = jnp.float32
BF16 = jnp.bfloat16
NN = (((1,), (0,)), ((), ()))
NT = (((1,), (1,)), ((), ()))


def halves(x):
    high = x.astype(BF16)
    return high, (x - high.astype(F32)).astype(BF16)


def product(a, b, dims):
    return lax.dot_general(a, b, dims, preferred_element_type=F32)


def dot3(a, b, dims):
    return product(a[0], b[0], dims) + (product(a[0], b[1], dims) + product(a[1], b[0], dims))


def stacked(b):
    return jnp.concatenate([b[0], b[0], b[1]], axis=0)


def dot_stacked(x, weights):
    high, low = halves(x)
    return product(jnp.concatenate([high, low, high], axis=1), weights, NN)


def kernel(
    n, group, z_ref, inverse_ref, couple_ref, coef_ref, anchor_ref, out_ref,
    tail_in, tail_out, upper_in, upper_out, enter_f, enter_b, solved_tail,
    map_f_in, map_f_out, map_b_in, map_b_out, left_in, right_in, left_out, right_out,
    top_rows, forward_w, backward_w, inv_hi, inv_lo, proj_hi, proj_lo, masked,
    sent, got, es, er,
):
    me = lax.axis_index("genome")
    count = n // group
    g, q = me // group, lax.rem(me, group)
    first, last = me == 0, me == n - 1
    head, tail = q == 0, q == group - 1
    start_group, end_group = g == 0, g == count - 1
    right, left = lax.rem(me + 1, n), lax.rem(me + n - 1, n)
    far_right, far_left = lax.rem(me + group, n), lax.rem(me + n - group, n)
    chunks, rows, half = tail_in.shape
    typed = inverse_ref.shape[0]
    top = typed - half
    traits = chunks * rows
    no = jnp.logical_not

    def both(*conditions):
        return functools.reduce(jnp.logical_and, conditions)

    barrier = pltpu.get_barrier_semaphore()
    for other in (left, right, far_left, far_right):
        pl.semaphore_signal(barrier, inc=1, device_id={"genome": other},
                            device_id_type=pl.DeviceIdType.MESH)

    def remote(src, dst, send, recv, other):
        return pltpu.make_async_remote_copy(
            src_ref=src, dst_ref=dst, send_sem=send, recv_sem=recv,
            device_id={"genome": other}, device_id_type=pl.DeviceIdType.MESH)

    def channel(index, src, dst, landing, other):
        return lambda c: remote(src.at[c], dst.at[c], sent.at[index, c], got.at[landing, c], other)

    map_f = channel(0, map_f_out, map_f_in, 0, right)
    local_f = channel(1, tail_out, tail_in, 1, right)
    group_f = channel(2, tail_out, enter_f, 2, far_right)
    pass_f = channel(3, enter_f, enter_f, 2, left)
    map_b = channel(4, map_b_out, map_b_in, 3, left)
    local_b = channel(5, upper_out, upper_in, 4, left)
    group_b = channel(6, upper_out, enter_b, 5, far_left)
    pass_b = channel(7, enter_b, enter_b, 5, right)

    def to_right():
        return remote(left_out, left_in, es.at[0], er.at[0], right)

    def to_left():
        return remote(right_out, right_in, es.at[1], er.at[1], left)

    def each(condition, step):
        @pl.when(condition)
        def _():
            def go(c, _):
                step(c)
                return 0
            lax.fori_loop(0, chunks, go, 0)

    def clear(condition, ref):
        @pl.when(condition)
        def _():
            ref[...] = jnp.zeros_like(ref)

    def unit(condition, ref):
        @pl.when(condition)
        def _():
            row = lax.broadcasted_iota(jnp.int32, (half, half), 0)
            col = lax.broadcasted_iota(jnp.int32, (half, half), 1)
            ref[...] = (row == col).astype(F32).reshape(ref.shape)

    hi, lo = halves(inverse_ref[...])
    inv_hi[...] = hi
    inv_lo[...] = lo
    z_halves = halves(z_ref[...])
    solved = dot3(z_halves, (inv_hi[pl.ds(top, half), :], inv_lo[pl.ds(top, half), :]), NT)
    tail_out[...] = solved.reshape(chunks, rows, half)
    solved_tail[...] = solved.reshape(chunks, rows, half)
    pl.semaphore_wait(barrier, 4)

    each(both(head, start_group, no(tail)), lambda c: local_f(c).start())

    projected = dot3((inv_hi[...], inv_lo[...]), halves(couple_ref[...]), NN)
    hi, lo = halves(projected)
    proj_hi[...] = hi
    proj_lo[...] = lo
    chain = -projected[top:, :]
    chain_t = chain.T
    map_f_out[...] = chain_t.reshape(map_f_out.shape)
    map_b_out[...] = chain.reshape(map_b_out.shape)
    forward_w[...] = stacked(halves(chain_t))
    backward_w[...] = stacked(halves(chain))

    def start_head(c):
        map_f(c).start()
    each(both(head, no(start_group), no(tail)), start_head)
    each(both(head, no(start_group), no(tail)), lambda c: local_f(c).start())
    each(both(tail, no(end_group), no(head)), lambda c: map_b(c).start())

    clear(head, tail_in)
    clear(tail, upper_in)
    clear(start_group, enter_f)
    clear(end_group, enter_b)
    clear(first, left_in)
    clear(last, right_in)
    unit(jnp.logical_or(head, start_group), map_f_in)
    unit(jnp.logical_or(tail, end_group), map_b_in)

    def step(c):
        map_f(c).wait_recv()
        map_f_out[c] = dot_stacked(map_f_in[c], forward_w[...])

        @pl.when(no(tail))
        def _():
            map_f(c).start()
    each(both(no(start_group), no(head)), step)

    def step(c):
        local_f(c).wait_recv()
        tail_out[c] = tail_out[c] + dot_stacked(tail_in[c], forward_w[...])

        @pl.when(no(tail))
        def _():
            local_f(c).start()

        @pl.when(both(tail, start_group, no(end_group)))
        def _():
            group_f(c).start()
    each(no(head), step)
    if group == 1:
        each(both(start_group, no(end_group)), lambda c: group_f(c).start())

    solved_top = dot3(z_halves, (inv_hi[pl.ds(0, top), :], inv_lo[pl.ds(0, top), :]), NT)
    top_rows[...] = solved_top.reshape(chunks, rows, top)

    def step(c):
        map_b(c).wait_recv()
        map_b_out[c] = dot_stacked(map_b_in[c], backward_w[...])

        @pl.when(no(head))
        def _():
            map_b(c).start()
    each(both(no(end_group), no(tail)), step)

    def make_mask():
        spread = 128
        units = anchor_ref.shape[1]
        nearest = jnp.broadcast_to(anchor_ref[...], (spread, units)).T
        start = me * typed - half
        lanes = lax.broadcasted_iota(jnp.int32, (units, spread), 1)
        for j in range(0, typed + 2 * half, spread):
            within = jnp.abs(lanes + (start + j) - nearest) <= half
            coef = coef_ref[:, j:j + spread].astype(F32)
            masked[:, j:j + spread] = jnp.where(within, coef, 0.0).astype(BF16)

    @pl.when(g >= count // 2)
    def _():
        make_mask()

    @pl.when(both(no(start_group), tail))
    def _():
        whole = stacked(halves(map_f_out[...].reshape(half, half)))

        def go(c, _):
            group_f(c).wait_recv()

            if group > 1:
                pass_f(c).start()
            tail_out[c] = tail_out[c] + dot_stacked(enter_f[c], whole)

            @pl.when(no(end_group))
            def _():
                group_f(c).start()
            return 0
        lax.fori_loop(0, chunks, go, 0)

    def step(c):
        pass_f(c).wait_recv()

        @pl.when(no(head))
        def _():
            pass_f(c).start()
    each(both(no(start_group), no(tail)), step)

    before = tail_in[...].reshape(traits, half) + dot_stacked(
        enter_f[...].reshape(traits, half), stacked(halves(map_f_in[...].reshape(half, half))))
    below = solved_tail[...].reshape(traits, half) + dot_stacked(before, forward_w[...])
    above = top_rows[...].reshape(traits, top) - dot3(
        halves(before), (proj_hi[pl.ds(0, top), :], proj_lo[pl.ds(0, top), :]), NT)
    add = dot3(halves(jnp.concatenate([above, below], axis=1)), (proj_hi[...], proj_lo[...]), NN)
    upper_out[...] = add.reshape(chunks, rows, half)
    each(both(tail, no(head)), lambda c: local_b(c).start())
    solved_tail[...] = below.reshape(chunks, rows, half)
    top_rows[...] = above.reshape(chunks, rows, top)

    def step(c):
        local_b(c).wait_recv()
        upper_out[c] = upper_out[c] + dot_stacked(upper_in[c], backward_w[...])

        @pl.when(no(head))
        def _():
            local_b(c).start()

        @pl.when(both(head, end_group, no(start_group)))
        def _():
            group_b(c).start()
    each(no(tail), step)
    if group == 1:
        each(both(end_group, no(start_group)), lambda c: group_b(c).start())

    @pl.when(both(no(end_group), head))
    def _():
        whole = stacked(halves(map_b_out[...].reshape(half, half)))

        def go(c, _):
            group_b(c).wait_recv()

            if group > 1:
                pass_b(c).start()

            @pl.when(no(start_group))
            def _():
                upper_out[c] = upper_out[c] + dot_stacked(enter_b[c], whole)
                group_b(c).start()
            return 0
        lax.fori_loop(0, chunks, go, 0)

    @pl.when(g < count // 2)
    def _():
        make_mask()

    def step(c):
        pass_b(c).wait_recv()

        @pl.when(no(tail))
        def _():
            pass_b(c).start()
    each(both(no(end_group), no(head)), step)

    after = upper_in[...].reshape(traits, half) + dot_stacked(
        enter_b[...].reshape(traits, half), stacked(halves(map_b_in[...].reshape(half, half))))
    rows_now = jnp.concatenate(
        [top_rows[...].reshape(traits, top), solved_tail[...].reshape(traits, half) - after], axis=1)
    weights = dot3(halves(rows_now), (inv_hi[...], inv_lo[...]), NN).astype(BF16)
    left_out[...] = weights[:, top:]
    right_out[...] = weights[:, :half]

    @pl.when(no(last))
    def _():
        to_right().start()

    @pl.when(no(first))
    def _():
        to_left().start()

    out_ref[...] = product(weights, masked[:, half:half + typed], NT)

    @pl.when(no(last))
    def _():
        to_left().wait_recv()

    out_ref[...] += product(right_in[...], masked[:, half + typed:], NT)

    @pl.when(no(first))
    def _():
        to_right().wait_recv()

    out_ref[...] += product(left_in[...], masked[:, :half], NT)

    each(both(no(start_group), no(tail)), lambda c: map_f(c).wait_send())
    each(no(tail), lambda c: local_f(c).wait_send())
    each(both(tail, no(end_group)), lambda c: group_f(c).wait_send())
    each(both(no(head), no(start_group)), lambda c: pass_f(c).wait_send())
    each(both(no(end_group), no(head)), lambda c: map_b(c).wait_send())
    each(no(head), lambda c: local_b(c).wait_send())
    each(both(head, no(start_group)), lambda c: group_b(c).wait_send())
    each(both(no(tail), no(end_group)), lambda c: pass_b(c).wait_send())

    @pl.when(no(last))
    def _():
        to_right().wait_send()

    @pl.when(no(first))
    def _():
        to_left().wait_send()


def per_device(n, z_typed, diag_inverse, coupling, impute_coef, anchor):
    traits, typed = z_typed.shape
    half = coupling.shape[2]
    units, span = impute_coef.shape
    top = typed - half
    chunks = next(k for k in (8, 4, 2, 1) if traits % (16 * k) == half % (8 * k) == 0 or k == 1)
    rows = traits // chunks
    group = 1
    while n % (2 * group) == 0 and 4 * group * group <= n:
        group *= 2
    state = pltpu.VMEM((chunks, rows, half), F32)
    edge = pltpu.VMEM((traits, half), BF16)
    chain_map = pltpu.VMEM((chunks, half // chunks, half), F32)
    return pl.pallas_call(
        functools.partial(kernel, n, group),
        out_shape=jax.ShapeDtypeStruct((traits, units), F32),
        in_specs=[pl.BlockSpec(memory_space=pltpu.VMEM)] * 5,
        out_specs=pl.BlockSpec(memory_space=pltpu.VMEM),
        scratch_shapes=[
            state, state, state, state, state, state, state,
            chain_map, chain_map, chain_map, chain_map, edge, edge, edge, edge,
            pltpu.VMEM((chunks, rows, top), F32),
            pltpu.VMEM((3 * half, half), BF16), pltpu.VMEM((3 * half, half), BF16),
            pltpu.VMEM((typed, typed), BF16), pltpu.VMEM((typed, typed), BF16),
            pltpu.VMEM((typed, half), BF16), pltpu.VMEM((typed, half), BF16),
            pltpu.VMEM((units, span), BF16),
            pltpu.SemaphoreType.DMA((8, chunks)), pltpu.SemaphoreType.DMA((6, chunks)),
            pltpu.SemaphoreType.DMA((2,)), pltpu.SemaphoreType.DMA((2,)),
        ],
        compiler_params=pltpu.CompilerParams(
            collective_id=0, has_side_effects=True, vmem_limit_bytes=48 * 1024 * 1024),
    )(z_typed, diag_inverse[0], coupling[0], impute_coef, anchor.reshape(1, units))


def solution(mesh):
    shared = ("seg", "genome")
    in_specs = (P(None, shared), P(shared, None, None), P(shared, None, None),
                P(shared, None), P(shared))
    return jax.shard_map(
        functools.partial(per_device, mesh.shape["genome"]), mesh=mesh, in_specs=in_specs,
        out_specs=P(None, shared), check_vma=False)
```

```python
import functools

import jax
import jax.numpy as jnp
from jax import lax
from jax.experimental import pallas as pl
from jax.experimental.pallas import tpu as pltpu
from jax.sharding import PartitionSpec as P

F32 = jnp.float32
BF16 = jnp.bfloat16
NN = (((1,), (0,)), ((), ()))
NT = (((1,), (1,)), ((), ()))


def halves(x):
    high = x.astype(BF16)
    return high, (x - high.astype(F32)).astype(BF16)


def product(a, b, dims):
    return lax.dot_general(a, b, dims, preferred_element_type=F32)


def dot3(a, b, dims):
    return product(a[0], b[0], dims) + (product(a[0], b[1], dims) + product(a[1], b[0], dims))


def stacked(b):
    return jnp.concatenate([b[0], b[0], b[1]], axis=0)


def dot_stacked(x, weights):
    high, low = halves(x)
    return product(jnp.concatenate([high, low, high], axis=1), weights, NN)


def kernel(
    n, group, z_hbm, inverse_hbm, couple_hbm, coef_hbm, anchor_hbm, out_ref,
    z_ref, inverse_ref, couple_ref, coef_ref, anchor_ref, fetched,
    tail_in, tail_out, upper_in, upper_out, enter_f, enter_b, carry_f,
    map_f_in, map_f_out, map_b_in, map_b_out, left_in, right_in, left_out, right_out,
    top_rows, base, enter_rows_w, enter_add_w, enter_base_w, forward_w, backward_w, inv_hi, inv_lo, proj_hi, proj_lo, masked,
    sent, got, es, er,
):
    me = lax.axis_index("genome")
    count = n // group
    g, q = me // group, lax.rem(me, group)
    first, last = me == 0, me == n - 1
    head, tail = q == 0, q == group - 1
    start_group, end_group = g == 0, g == count - 1
    right, left = lax.rem(me + 1, n), lax.rem(me + n - 1, n)
    far_right, far_left = lax.rem(me + group, n), lax.rem(me + n - group, n)
    chunks, rows, half = tail_in.shape
    typed = inverse_ref.shape[0]
    top = typed - half
    traits = chunks * rows
    no = jnp.logical_not
    even = lax.rem(q, 2) == 0
    fetch = [
        pltpu.make_async_copy(src, dst, fetched.at[i])
        for i, (src, dst) in enumerate((
            (inverse_hbm, inverse_ref), (z_hbm, z_ref), (couple_hbm, couple_ref),
            (anchor_hbm, anchor_ref), (coef_hbm, coef_ref)))]
    for copy in fetch:
        copy.start()

    def both(*conditions):
        return functools.reduce(jnp.logical_and, conditions)

    barrier = pltpu.get_barrier_semaphore()
    right_two, left_two = lax.rem(me + 2, n), lax.rem(me + n - 2, n)
    for other in (left, right, left_two, right_two, far_left, far_right):
        pl.semaphore_signal(barrier, inc=1, device_id={"genome": other},
                            device_id_type=pl.DeviceIdType.MESH)

    def remote(src, dst, send, recv, other):
        return pltpu.make_async_remote_copy(
            src_ref=src, dst_ref=dst, send_sem=send, recv_sem=recv,
            device_id={"genome": other}, device_id_type=pl.DeviceIdType.MESH)

    def channel(index, src, dst, landing, other):
        return lambda c: remote(src.at[c], dst.at[c], sent.at[index, c], got.at[landing, c], other)

    map_f = channel(0, map_f_out, map_f_in, 0, right)
    local_f = channel(1, tail_out, tail_in, 1, right)
    group_f = channel(2, carry_f, enter_f, 2, far_right)
    pass_f = channel(3, enter_f, enter_f, 2, left)
    map_b = channel(4, map_b_out, map_b_in, 3, left)
    local_b = channel(5, upper_out, upper_in, 4, left)
    group_b = channel(6, upper_out, enter_b, 5, far_left)
    pass_b = channel(7, enter_b, enter_b, 5, right)
    pass_f_two = channel(8, enter_f, enter_f, 2, left_two)
    pass_b_two = channel(9, enter_b, enter_b, 5, right_two)

    def pass_on_f(c):
        @pl.when(no(even))
        def _():
            pass_f(c).start()

        @pl.when(both(no(even), q >= 2))
        def _():
            pass_f_two(c).start()

    def pass_on_b(c):
        @pl.when(both(even, q + 1 < group))
        def _():
            pass_b(c).start()

        @pl.when(both(even, q + 2 < group))
        def _():
            pass_b_two(c).start()

    def to_right():
        return remote(left_out, left_in, es.at[0], er.at[0], right)

    def to_left():
        return remote(right_out, right_in, es.at[1], er.at[1], left)

    def each(condition, step):
        @pl.when(condition)
        def _():
            def go(c, _):
                step(c)
                return 0
            lax.fori_loop(0, chunks, go, 0)

    def clear(condition, ref):
        @pl.when(condition)
        def _():
            ref[...] = jnp.zeros_like(ref)

    def unit(condition, ref):
        @pl.when(condition)
        def _():
            row = lax.broadcasted_iota(jnp.int32, (half, half), 0)
            col = lax.broadcasted_iota(jnp.int32, (half, half), 1)
            ref[...] = (row == col).astype(F32).reshape(ref.shape)

    fetch[0].wait()
    hi, lo = halves(inverse_ref[...])
    inv_hi[...] = hi
    inv_lo[...] = lo
    fetch[1].wait()
    z_halves = halves(z_ref[...])
    solved = dot3(z_halves, (inv_hi[pl.ds(top, half), :], inv_lo[pl.ds(top, half), :]), NT)
    tail_out[...] = solved.reshape(chunks, rows, half)
    pl.semaphore_wait(barrier, 6)

    each(both(head, start_group, no(tail)), lambda c: local_f(c).start())

    fetch[2].wait()
    projected = dot3((inv_hi[...], inv_lo[...]), halves(couple_ref[...]), NN)
    hi, lo = halves(projected)
    proj_hi[...] = hi
    proj_lo[...] = lo
    chain = -projected[top:, :]
    chain_t = chain.T
    map_f_out[...] = chain_t.reshape(map_f_out.shape)
    map_b_out[...] = chain.reshape(map_b_out.shape)
    forward_w[...] = stacked(halves(chain_t))
    backward_w[...] = stacked(halves(chain))

    def start_head(c):
        map_f(c).start()
    each(both(head, no(start_group), no(tail)), start_head)
    each(both(head, no(start_group), no(tail)), lambda c: local_f(c).start())
    each(both(tail, no(end_group), no(head)), lambda c: map_b(c).start())

    clear(head, tail_in)
    clear(tail, upper_in)
    clear(start_group, enter_f)
    clear(end_group, enter_b)
    clear(first, left_in)
    clear(last, right_in)
    unit(jnp.logical_or(head, start_group), map_f_in)
    unit(jnp.logical_or(tail, end_group), map_b_in)

    def step(c):
        map_f(c).wait_recv()
        map_f_out[c] = dot_stacked(map_f_in[c], forward_w[...])

        @pl.when(no(tail))
        def _():
            map_f(c).start()
    each(both(no(start_group), no(head)), step)

    def step(c):
        local_f(c).wait_recv()
        tail_out[c] = tail_out[c] + dot_stacked(tail_in[c], forward_w[...])

        @pl.when(no(tail))
        def _():
            local_f(c).start()

        @pl.when(both(tail, start_group, no(end_group)))
        def _():
            carry_f[c] = tail_out[c]
            group_f(c).start()
    each(no(head), step)
    if group == 1:
        def step(c):
            carry_f[c] = tail_out[c]
            group_f(c).start()
        each(both(start_group, no(end_group)), step)

    solved_top = dot3(z_halves, (inv_hi[pl.ds(0, top), :], inv_lo[pl.ds(0, top), :]), NT)
    top_rows[...] = solved_top.reshape(chunks, rows, top)

    def step(c):
        map_b(c).wait_recv()
        map_b_out[c] = dot_stacked(map_b_in[c], backward_w[...])

        @pl.when(no(head))
        def _():
            map_b(c).start()
    each(both(no(end_group), no(tail)), step)

    fetch[3].wait()
    fetch[4].wait()

    def make_mask():
        spread = 128
        units = anchor_ref.shape[1]
        nearest = jnp.broadcast_to(anchor_ref[...], (spread, units)).T
        start = me * typed - half
        lanes = lax.broadcasted_iota(jnp.int32, (units, spread), 1)
        for j in range(0, typed + 2 * half, spread):
            within = jnp.abs(lanes + (start + j) - nearest) <= half
            coef = coef_ref[:, j:j + spread].astype(F32)
            masked[:, j:j + spread] = jnp.where(within, coef, 0.0).astype(BF16)

    @pl.when(g >= count // 2)
    def _():
        make_mask()

    def prepare():
        proj = (proj_hi[...], proj_lo[...])
        proj_top = (proj_hi[pl.ds(0, top), :], proj_lo[pl.ds(0, top), :])
        above = top_rows[...].reshape(traits, top) - dot3(
            halves(tail_in[...].reshape(traits, half)), proj_top, NT)
        top_rows[...] = above.reshape(chunks, rows, top)
        all_rows = jnp.concatenate([above, tail_out[...].reshape(traits, half)], axis=1)
        upper_out[...] = dot3(halves(all_rows), proj, NN).reshape(chunks, rows, half)

        @pl.when(no(start_group))
        def _():
            slope_top = -dot3(halves(map_f_in[...].reshape(half, half)), proj_top, NT)
            slope = jnp.concatenate([slope_top, map_f_out[...].reshape(half, half)], axis=1)
            slope_halves = halves(slope)
            enter_rows_w[...] = stacked(slope_halves)
            enter_add_w[...] = stacked(halves(dot3(slope_halves, proj, NN)))

    relay = both(no(start_group), no(end_group), tail)

    @pl.when(no(relay))
    def _():
        prepare()

    @pl.when(relay)
    def _():
        whole = stacked(halves(map_f_out[...].reshape(half, half)))

        def go(c, _):
            group_f(c).wait_recv()
            pass_on_f(c)
            carry_f[c] = tail_out[c] + dot_stacked(enter_f[c], whole)
            group_f(c).start()
            return 0
        lax.fori_loop(0, chunks, go, 0)
        prepare()

    def step(c):
        group_f(c).wait_recv()
        pass_on_f(c)
    each(both(no(start_group), no(end_group), no(tail)), step)

    @pl.when(both(no(start_group), no(end_group)))
    def _():
        add = dot_stacked(enter_f[...].reshape(traits, half), enter_add_w[...])
        upper_out[...] += add.reshape(chunks, rows, half)

    each(both(tail, no(head), no(end_group)), lambda c: local_b(c).start())

    def step(c):
        local_b(c).wait_recv()
        upper_out[c] = upper_out[c] + dot_stacked(upper_in[c], backward_w[...])

        @pl.when(no(head))
        def _():
            local_b(c).start()
    each(both(no(tail), no(end_group)), step)

    def step(c):
        @pl.when(no(start_group))
        def _():
            group_f(c).wait_recv()
            pass_on_f(c)
            upper_out[c] = upper_out[c] + dot_stacked(enter_f[c], enter_add_w[...])

        @pl.when(no(tail))
        def _():
            local_b(c).wait_recv()
            upper_out[c] = upper_out[c] + dot_stacked(upper_in[c], backward_w[...])

        @pl.when(no(head))
        def _():
            local_b(c).start()

        @pl.when(both(head, no(start_group)))
        def _():
            group_b(c).start()
    each(end_group, step)

    all_rows = jnp.concatenate([top_rows[...].reshape(traits, top),
                                tail_out[...].reshape(traits, half)], axis=1)
    base[...] = all_rows

    @pl.when(no(start_group))
    def _():
        base[...] += dot_stacked(enter_f[...].reshape(traits, half), enter_rows_w[...])

    base[:, top:] -= upper_in[...].reshape(traits, half)
    base[...] = dot3(halves(base[...]), (inv_hi[...], inv_lo[...]), NN)

    @pl.when(no(end_group))
    def _():
        slope = dot3(halves(map_b_in[...].reshape(half, half)),
                     (inv_hi[pl.ds(top, half), :], inv_lo[pl.ds(top, half), :]), NN)
        enter_base_w[...] = stacked(halves(slope))

    @pl.when(g < count // 2)
    def _():
        make_mask()

    @pl.when(both(no(end_group), head))
    def _():
        whole = stacked(halves(map_b_out[...].reshape(half, half)))

        def go(c, _):
            group_b(c).wait_recv()
            pass_on_b(c)

            @pl.when(no(start_group))
            def _():
                upper_out[c] = upper_out[c] + dot_stacked(enter_b[c], whole)
                group_b(c).start()
            return 0
        lax.fori_loop(0, chunks, go, 0)

    def step(c):
        group_b(c).wait_recv()
        pass_on_b(c)
    each(both(no(end_group), no(head)), step)

    @pl.when(no(end_group))
    def _():
        base[...] -= dot_stacked(enter_b[...].reshape(traits, half), enter_base_w[...])

    weights = base[...].astype(BF16)
    left_out[...] = weights[:, top:]
    right_out[...] = weights[:, :half]

    @pl.when(no(last))
    def _():
        to_right().start()

    @pl.when(no(first))
    def _():
        to_left().start()

    out_ref[...] = product(weights, masked[:, half:half + typed], NT)

    @pl.when(no(last))
    def _():
        to_left().wait_recv()

    out_ref[...] += product(right_in[...], masked[:, half + typed:], NT)

    @pl.when(no(first))
    def _():
        to_right().wait_recv()

    out_ref[...] += product(left_in[...], masked[:, :half], NT)

    each(both(no(start_group), no(tail)), lambda c: map_f(c).wait_send())
    each(no(tail), lambda c: local_f(c).wait_send())
    each(both(tail, no(end_group)), lambda c: group_f(c).wait_send())
    each(both(no(even), no(start_group)), lambda c: pass_f(c).wait_send())
    each(both(no(even), q >= 2, no(start_group)), lambda c: pass_f_two(c).wait_send())
    each(both(no(end_group), no(head)), lambda c: map_b(c).wait_send())
    each(no(head), lambda c: local_b(c).wait_send())
    each(both(head, no(start_group)), lambda c: group_b(c).wait_send())
    each(both(even, q + 1 < group, no(end_group)), lambda c: pass_b(c).wait_send())
    each(both(even, q + 2 < group, no(end_group)), lambda c: pass_b_two(c).wait_send())

    @pl.when(no(last))
    def _():
        to_right().wait_send()

    @pl.when(no(first))
    def _():
        to_left().wait_send()


def per_device(n, z_typed, diag_inverse, coupling, impute_coef, anchor):
    traits, typed = z_typed.shape
    half = coupling.shape[2]
    units, span = impute_coef.shape
    top = typed - half
    chunks = next(k for k in (8, 4, 2, 1) if traits % (16 * k) == half % (8 * k) == 0 or k == 1)
    rows = traits // chunks
    group = 1
    while n % (2 * group) == 0 and 4 * group * group <= n:
        group *= 2
    state = pltpu.VMEM((chunks, rows, half), F32)
    edge = pltpu.VMEM((traits, half), BF16)
    chain_map = pltpu.VMEM((chunks, half // chunks, half), F32)
    return pl.pallas_call(
        functools.partial(kernel, n, group),
        out_shape=jax.ShapeDtypeStruct((traits, units), F32),
        in_specs=[pl.BlockSpec(memory_space=pltpu.HBM)] * 5,
        out_specs=pl.BlockSpec(memory_space=pltpu.VMEM),
        scratch_shapes=[
            pltpu.VMEM((traits, typed), F32), pltpu.VMEM((typed, typed), F32),
            pltpu.VMEM((typed, half), F32), pltpu.VMEM((units, span), BF16),
            pltpu.VMEM((1, units), jnp.int32), pltpu.SemaphoreType.DMA((5,)),
            state, state, state, state, state, state, state,
            chain_map, chain_map, chain_map, chain_map, edge, edge, edge, edge,
            pltpu.VMEM((chunks, rows, top), F32), pltpu.VMEM((traits, typed), F32),
            pltpu.VMEM((3 * half, typed), BF16), pltpu.VMEM((3 * half, half), BF16),
            pltpu.VMEM((3 * half, typed), BF16),
            pltpu.VMEM((3 * half, half), BF16), pltpu.VMEM((3 * half, half), BF16),
            pltpu.VMEM((typed, typed), BF16), pltpu.VMEM((typed, typed), BF16),
            pltpu.VMEM((typed, half), BF16), pltpu.VMEM((typed, half), BF16),
            pltpu.VMEM((units, span), BF16),
            pltpu.SemaphoreType.DMA((10, chunks)), pltpu.SemaphoreType.DMA((6, chunks)),
            pltpu.SemaphoreType.DMA((2,)), pltpu.SemaphoreType.DMA((2,)),
        ],
        compiler_params=pltpu.CompilerParams(
            collective_id=0, has_side_effects=True, vmem_limit_bytes=63 * 1024 * 1024),
    )(z_typed, diag_inverse[0], coupling[0], impute_coef, anchor.reshape(1, units))


def solution(mesh):
    shared = ("seg", "genome")
    in_specs = (P(None, shared), P(shared, None, None), P(shared, None, None),
                P(shared, None), P(shared))
    return jax.shard_map(
        functools.partial(per_device, mesh.shape["genome"]), mesh=mesh, in_specs=in_specs,
        out_specs=P(None, shared), check_vma=False)
```

```python
import functools

import jax
import jax.numpy as jnp
from jax import lax
from jax.experimental import pallas as pl
from jax.experimental.pallas import tpu as pltpu
from jax.sharding import PartitionSpec as P

F32 = jnp.float32
BF16 = jnp.bfloat16
NN = (((1,), (0,)), ((), ()))
NT = (((1,), (1,)), ((), ()))


def halves(x):
    high = x.astype(BF16)
    return high, (x - high.astype(F32)).astype(BF16)


def product(a, b, dims):
    return lax.dot_general(a, b, dims, preferred_element_type=F32)


def dot3(a, b, dims):
    return product(a[0], b[0], dims) + (product(a[0], b[1], dims) + product(a[1], b[0], dims))


def stacked(b):
    return jnp.concatenate([b[0], b[0], b[1]], axis=0)


def dot_stacked(x, weights):
    high, low = halves(x)
    return product(jnp.concatenate([high, low, high], axis=1), weights, NN)


def kernel(
    n, group, z_hbm, inverse_hbm, couple_hbm, coef_hbm, anchor_hbm, out_ref,
    z_ref, inverse_ref, couple_ref, coef_ref, anchor_ref, fetched,
    tail_in, tail_out, upper_in, upper_out, enter_f, enter_b, carry_f,
    map_f_in, map_f_out, map_b_in, map_b_out, left_in, right_in, left_out, right_out,
    top_rows, base, enter_rows_w, enter_add_w, enter_base_w, forward_w, backward_w, inv_hi, inv_lo, proj_hi, proj_lo, masked,
    sent, got, es, er,
):
    me = lax.axis_index("genome")
    count = n // group
    g, q = me // group, lax.rem(me, group)
    first, last = me == 0, me == n - 1
    head, tail = q == 0, q == group - 1
    start_group, end_group = g == 0, g == count - 1
    right, left = lax.rem(me + 1, n), lax.rem(me + n - 1, n)
    far_right, far_left = lax.rem(me + group, n), lax.rem(me + n - group, n)
    chunks, rows, half = tail_in.shape
    typed = inverse_ref.shape[0]
    top = typed - half
    traits = chunks * rows
    no = jnp.logical_not
    even = lax.rem(q, 2) == 0
    fetch = [
        pltpu.make_async_copy(src, dst, fetched.at[i])
        for i, (src, dst) in enumerate((
            (inverse_hbm, inverse_ref), (z_hbm, z_ref), (couple_hbm, couple_ref),
            (anchor_hbm, anchor_ref), (coef_hbm, coef_ref)))]
    for copy in fetch:
        copy.start()

    def both(*conditions):
        return functools.reduce(jnp.logical_and, conditions)

    barrier = pltpu.get_barrier_semaphore()
    right_two, left_two = lax.rem(me + 2, n), lax.rem(me + n - 2, n)
    for other in (left, right, left_two, right_two, far_left, far_right):
        pl.semaphore_signal(barrier, inc=1, device_id={"genome": other},
                            device_id_type=pl.DeviceIdType.MESH)

    def remote(src, dst, send, recv, other):
        return pltpu.make_async_remote_copy(
            src_ref=src, dst_ref=dst, send_sem=send, recv_sem=recv,
            device_id={"genome": other}, device_id_type=pl.DeviceIdType.MESH)

    def channel(index, src, dst, landing, other):
        return lambda c: remote(src.at[c], dst.at[c], sent.at[index, c], got.at[landing, c], other)

    map_f = channel(0, map_f_out, map_f_in, 0, right)
    local_f = channel(1, tail_out, tail_in, 1, right)
    group_f = channel(2, carry_f, enter_f, 2, far_right)
    pass_f = channel(3, enter_f, enter_f, 2, left)
    map_b = channel(4, map_b_out, map_b_in, 3, left)
    local_b = channel(5, upper_out, upper_in, 4, left)
    group_b = channel(6, upper_out, enter_b, 5, far_left)
    pass_b = channel(7, enter_b, enter_b, 5, right)
    pass_f_two = channel(8, enter_f, enter_f, 2, left_two)
    pass_b_two = channel(9, enter_b, enter_b, 5, right_two)

    def pass_on_f(c):
        @pl.when(no(even))
        def _():
            pass_f(c).start()

        @pl.when(both(no(even), q >= 2))
        def _():
            pass_f_two(c).start()

    def pass_on_b(c):
        @pl.when(both(even, q + 1 < group))
        def _():
            pass_b(c).start()

        @pl.when(both(even, q + 2 < group))
        def _():
            pass_b_two(c).start()

    def to_right():
        return remote(left_out, left_in, es.at[0], er.at[0], right)

    def to_left():
        return remote(right_out, right_in, es.at[1], er.at[1], left)

    def each(condition, step):
        @pl.when(condition)
        def _():
            def go(c, _):
                step(c)
                return 0
            lax.fori_loop(0, chunks, go, 0)

    def clear(condition, ref):
        @pl.when(condition)
        def _():
            ref[...] = jnp.zeros_like(ref)

    def unit(condition, ref):
        @pl.when(condition)
        def _():
            row = lax.broadcasted_iota(jnp.int32, (half, half), 0)
            col = lax.broadcasted_iota(jnp.int32, (half, half), 1)
            ref[...] = (row == col).astype(F32).reshape(ref.shape)

    fetch[0].wait()
    hi, lo = halves(inverse_ref[...])
    inv_hi[...] = hi
    inv_lo[...] = lo
    fetch[1].wait()
    z_halves = halves(z_ref[...])
    solved = dot3(z_halves, (inv_hi[pl.ds(top, half), :], inv_lo[pl.ds(top, half), :]), NT)
    tail_out[...] = solved.reshape(chunks, rows, half)
    pl.semaphore_wait(barrier, 6)

    each(both(head, start_group, no(tail)), lambda c: local_f(c).start())

    fetch[2].wait()
    projected = dot3((inv_hi[...], inv_lo[...]), halves(couple_ref[...]), NN)
    hi, lo = halves(projected)
    proj_hi[...] = hi
    proj_lo[...] = lo
    chain = -projected[top:, :]
    chain_t = chain.T
    map_f_out[...] = chain_t.reshape(map_f_out.shape)
    map_b_out[...] = chain.reshape(map_b_out.shape)
    forward_w[...] = stacked(halves(chain_t))
    backward_w[...] = stacked(halves(chain))

    def start_head(c):
        map_f(c).start()
        local_f(c).start()
    each(both(head, no(start_group), no(tail)), start_head)
    each(both(tail, no(end_group), no(head)), lambda c: map_b(c).start())

    clear(head, tail_in)
    clear(tail, upper_in)
    clear(start_group, enter_f)
    clear(end_group, enter_b)
    clear(first, left_in)
    clear(last, right_in)
    unit(jnp.logical_or(head, start_group), map_f_in)
    unit(jnp.logical_or(tail, end_group), map_b_in)

    def step(c):
        map_f(c).wait_recv()
        local_f(c).wait_recv()
        moved = dot_stacked(jnp.concatenate([map_f_in[c], tail_in[c]], axis=0), forward_w[...])
        map_f_out[c] = moved[:half // chunks]
        tail_out[c] = tail_out[c] + moved[half // chunks:]

        @pl.when(no(tail))
        def _():
            map_f(c).start()
            local_f(c).start()
    each(both(no(start_group), no(head)), step)

    def step(c):
        local_f(c).wait_recv()
        tail_out[c] = tail_out[c] + dot_stacked(tail_in[c], forward_w[...])

        @pl.when(no(tail))
        def _():
            local_f(c).start()

        @pl.when(both(tail, start_group, no(end_group)))
        def _():
            carry_f[c] = tail_out[c]
            group_f(c).start()
    each(both(start_group, no(head)), step)
    if group == 1:
        def step(c):
            carry_f[c] = tail_out[c]
            group_f(c).start()
        each(both(start_group, no(end_group)), step)

    solved_top = dot3(z_halves, (inv_hi[pl.ds(0, top), :], inv_lo[pl.ds(0, top), :]), NT)
    top_rows[...] = solved_top.reshape(chunks, rows, top)

    def step(c):
        map_b(c).wait_recv()
        map_b_out[c] = dot_stacked(map_b_in[c], backward_w[...])

        @pl.when(no(head))
        def _():
            map_b(c).start()
    each(both(no(end_group), no(tail)), step)

    fetch[3].wait()
    fetch[4].wait()

    def make_mask():
        spread = 128
        units = anchor_ref.shape[1]
        nearest = jnp.broadcast_to(anchor_ref[...], (spread, units)).T
        start = me * typed - half
        lanes = lax.broadcasted_iota(jnp.int32, (units, spread), 1)
        for j in range(0, typed + 2 * half, spread):
            within = jnp.abs(lanes + (start + j) - nearest) <= half
            coef = coef_ref[:, j:j + spread].astype(F32)
            masked[:, j:j + spread] = jnp.where(within, coef, 0.0).astype(BF16)

    @pl.when(g >= count // 2)
    def _():
        make_mask()

    def prepare():
        proj = (proj_hi[...], proj_lo[...])
        proj_top = (proj_hi[pl.ds(0, top), :], proj_lo[pl.ds(0, top), :])
        above = top_rows[...].reshape(traits, top) - dot3(
            halves(tail_in[...].reshape(traits, half)), proj_top, NT)
        top_rows[...] = above.reshape(chunks, rows, top)
        all_rows = jnp.concatenate([above, tail_out[...].reshape(traits, half)], axis=1)
        upper_out[...] = dot3(halves(all_rows), proj, NN).reshape(chunks, rows, half)

        @pl.when(no(start_group))
        def _():
            slope_top = -dot3(halves(map_f_in[...].reshape(half, half)), proj_top, NT)
            slope = jnp.concatenate([slope_top, map_f_out[...].reshape(half, half)], axis=1)
            slope_halves = halves(slope)
            enter_rows_w[...] = stacked(slope_halves)
            enter_add_w[...] = stacked(halves(dot3(slope_halves, proj, NN)))

    relay = both(no(start_group), no(end_group), tail)

    @pl.when(no(relay))
    def _():
        prepare()

    @pl.when(relay)
    def _():
        whole = stacked(halves(map_f_out[...].reshape(half, half)))

        def go(c, _):
            group_f(c).wait_recv()
            pass_on_f(c)
            carry_f[c] = tail_out[c] + dot_stacked(enter_f[c], whole)
            group_f(c).start()
            return 0
        lax.fori_loop(0, chunks, go, 0)
        prepare()

    def step(c):
        group_f(c).wait_recv()
        pass_on_f(c)
    each(both(no(start_group), no(end_group), no(tail)), step)

    @pl.when(both(no(start_group), no(end_group)))
    def _():
        add = dot_stacked(enter_f[...].reshape(traits, half), enter_add_w[...])
        upper_out[...] += add.reshape(chunks, rows, half)

    each(both(tail, no(head), no(end_group)), lambda c: local_b(c).start())

    def step(c):
        local_b(c).wait_recv()
        upper_out[c] = upper_out[c] + dot_stacked(upper_in[c], backward_w[...])

        @pl.when(no(head))
        def _():
            local_b(c).start()
    each(both(no(tail), no(end_group)), step)

    def step(c):
        @pl.when(no(start_group))
        def _():
            group_f(c).wait_recv()
            pass_on_f(c)
            upper_out[c] = upper_out[c] + dot_stacked(enter_f[c], enter_add_w[...])

        @pl.when(no(tail))
        def _():
            local_b(c).wait_recv()
            upper_out[c] = upper_out[c] + dot_stacked(upper_in[c], backward_w[...])

        @pl.when(no(head))
        def _():
            local_b(c).start()

        @pl.when(both(head, no(start_group)))
        def _():
            group_b(c).start()
    each(end_group, step)

    all_rows = jnp.concatenate([top_rows[...].reshape(traits, top),
                                tail_out[...].reshape(traits, half)], axis=1)
    base[...] = all_rows

    @pl.when(no(start_group))
    def _():
        base[...] += dot_stacked(enter_f[...].reshape(traits, half), enter_rows_w[...])

    base[:, top:] -= upper_in[...].reshape(traits, half)
    base[...] = dot3(halves(base[...]), (inv_hi[...], inv_lo[...]), NN)

    @pl.when(no(end_group))
    def _():
        slope = dot3(halves(map_b_in[...].reshape(half, half)),
                     (inv_hi[pl.ds(top, half), :], inv_lo[pl.ds(top, half), :]), NN)
        enter_base_w[...] = stacked(halves(slope))

    @pl.when(g < count // 2)
    def _():
        make_mask()

    def drain_early():
        each(both(no(start_group), no(tail)), lambda c: map_f(c).wait_send())
        each(no(tail), lambda c: local_f(c).wait_send())
        each(both(tail, no(end_group)), lambda c: group_f(c).wait_send())
        each(both(no(even), no(start_group)), lambda c: pass_f(c).wait_send())
        each(both(no(even), q >= 2, no(start_group)), lambda c: pass_f_two(c).wait_send())
        each(both(no(end_group), no(head)), lambda c: map_b(c).wait_send())
        each(no(head), lambda c: local_b(c).wait_send())

    @pl.when(g < count // 2)
    def _():
        drain_early()

    @pl.when(both(no(end_group), head))
    def _():
        whole = stacked(halves(map_b_out[...].reshape(half, half)))

        def go(c, _):
            group_b(c).wait_recv()
            pass_on_b(c)

            @pl.when(no(start_group))
            def _():
                upper_out[c] = upper_out[c] + dot_stacked(enter_b[c], whole)
                group_b(c).start()
            return 0
        lax.fori_loop(0, chunks, go, 0)

    def step(c):
        group_b(c).wait_recv()
        pass_on_b(c)
    each(both(no(end_group), no(head)), step)

    @pl.when(no(end_group))
    def _():
        base[...] -= dot_stacked(enter_b[...].reshape(traits, half), enter_base_w[...])

    weights = base[...].astype(BF16)
    left_out[...] = weights[:, top:]
    right_out[...] = weights[:, :half]

    @pl.when(no(last))
    def _():
        to_right().start()

    @pl.when(no(first))
    def _():
        to_left().start()

    out_ref[...] = product(weights, masked[:, half:half + typed], NT)

    @pl.when(no(last))
    def _():
        to_left().wait_recv()

    out_ref[...] += product(right_in[...], masked[:, half + typed:], NT)

    @pl.when(no(first))
    def _():
        to_right().wait_recv()

    out_ref[...] += product(left_in[...], masked[:, :half], NT)

    @pl.when(g >= count // 2)
    def _():
        drain_early()

    each(both(head, no(start_group)), lambda c: group_b(c).wait_send())
    each(both(even, q + 1 < group, no(end_group)), lambda c: pass_b(c).wait_send())
    each(both(even, q + 2 < group, no(end_group)), lambda c: pass_b_two(c).wait_send())

    @pl.when(no(last))
    def _():
        to_right().wait_send()

    @pl.when(no(first))
    def _():
        to_left().wait_send()


def per_device(n, z_typed, diag_inverse, coupling, impute_coef, anchor):
    traits, typed = z_typed.shape
    half = coupling.shape[2]
    units, span = impute_coef.shape
    top = typed - half
    chunks = next(k for k in (8, 4, 2, 1) if traits % (16 * k) == half % (8 * k) == 0 or k == 1)
    rows = traits // chunks
    group = 1
    while n % (2 * group) == 0 and 4 * group * group <= n:
        group *= 2
    state = pltpu.VMEM((chunks, rows, half), F32)
    edge = pltpu.VMEM((traits, half), BF16)
    chain_map = pltpu.VMEM((chunks, half // chunks, half), F32)
    return pl.pallas_call(
        functools.partial(kernel, n, group),
        out_shape=jax.ShapeDtypeStruct((traits, units), F32),
        in_specs=[pl.BlockSpec(memory_space=pltpu.HBM)] * 5,
        out_specs=pl.BlockSpec(memory_space=pltpu.VMEM),
        scratch_shapes=[
            pltpu.VMEM((traits, typed), F32), pltpu.VMEM((typed, typed), F32),
            pltpu.VMEM((typed, half), F32), pltpu.VMEM((units, span), BF16),
            pltpu.VMEM((1, units), jnp.int32), pltpu.SemaphoreType.DMA((5,)),
            state, state, state, state, state, state, state,
            chain_map, chain_map, chain_map, chain_map, edge, edge, edge, edge,
            pltpu.VMEM((chunks, rows, top), F32), pltpu.VMEM((traits, typed), F32),
            pltpu.VMEM((3 * half, typed), BF16), pltpu.VMEM((3 * half, half), BF16),
            pltpu.VMEM((3 * half, typed), BF16),
            pltpu.VMEM((3 * half, half), BF16), pltpu.VMEM((3 * half, half), BF16),
            pltpu.VMEM((typed, typed), BF16), pltpu.VMEM((typed, typed), BF16),
            pltpu.VMEM((typed, half), BF16), pltpu.VMEM((typed, half), BF16),
            pltpu.VMEM((units, span), BF16),
            pltpu.SemaphoreType.DMA((10, chunks)), pltpu.SemaphoreType.DMA((6, chunks)),
            pltpu.SemaphoreType.DMA((2,)), pltpu.SemaphoreType.DMA((2,)),
        ],
        compiler_params=pltpu.CompilerParams(
            collective_id=0, has_side_effects=True, vmem_limit_bytes=63 * 1024 * 1024),
    )(z_typed, diag_inverse[0], coupling[0], impute_coef, anchor.reshape(1, units))


def solution(mesh):
    shared = ("seg", "genome")
    in_specs = (P(None, shared), P(shared, None, None), P(shared, None, None),
                P(shared, None), P(shared))
    return jax.shard_map(
        functools.partial(per_device, mesh.shape["genome"]), mesh=mesh, in_specs=in_specs,
        out_specs=P(None, shared), check_vma=False)
```

```python
import functools

import jax
import jax.numpy as jnp
from jax import lax
from jax.experimental import pallas as pl
from jax.experimental.pallas import tpu as pltpu
from jax.sharding import PartitionSpec as P

F32 = jnp.float32
BF16 = jnp.bfloat16
NN = (((1,), (0,)), ((), ()))
NT = (((1,), (1,)), ((), ()))


def halves(x):
    high = x.astype(BF16)
    return high, (x - high.astype(F32)).astype(BF16)


def product(a, b, dims):
    return lax.dot_general(a, b, dims, preferred_element_type=F32)


def dot3(a, b, dims):
    return product(a[0], b[0], dims) + (product(a[0], b[1], dims) + product(a[1], b[0], dims))


def stacked(b):
    return jnp.concatenate([b[0], b[0], b[1]], axis=0)


def dot_stacked(x, weights):
    high, low = halves(x)
    return product(jnp.concatenate([high, low, high], axis=1), weights, NN)


def kernel(
    n, group, z_hbm, inverse_hbm, couple_hbm, coef_hbm, anchor_hbm, out_ref,
    z_ref, inverse_ref, couple_ref, coef_ref, anchor_ref, fetched,
    tail_in, tail_out, upper_in, upper_out, enter_f, enter_b, carry_f,
    map_f_in, map_f_out, map_b_in, map_b_out, left_in, right_in, left_out, right_out,
    top_rows, base, enter_rows_w, enter_add_w, enter_base_w, forward_w, backward_w, inv_hi, inv_lo, proj_hi, proj_lo, masked,
    pre_base_out, pre_base_in, pre_slope_out, pre_slope_in, ps, pr,
    sent, got, es, er,
):
    me = lax.axis_index("genome")
    count = n // group
    g, q = me // group, lax.rem(me, group)
    first, last = me == 0, me == n - 1
    head, tail = q == 0, q == group - 1
    start_group, end_group = g == 0, g == count - 1
    right, left = lax.rem(me + 1, n), lax.rem(me + n - 1, n)
    far_right, far_left = lax.rem(me + group, n), lax.rem(me + n - group, n)
    chunks, rows, half = tail_in.shape
    typed = inverse_ref.shape[0]
    top = typed - half
    traits = chunks * rows
    no = jnp.logical_not
    even = lax.rem(q, 2) == 0
    fetch = [
        pltpu.make_async_copy(src, dst, fetched.at[i])
        for i, (src, dst) in enumerate((
            (inverse_hbm, inverse_ref), (z_hbm, z_ref), (couple_hbm, couple_ref),
            (anchor_hbm, anchor_ref), (coef_hbm, coef_ref)))]
    for copy in fetch:
        copy.start()

    def both(*conditions):
        return functools.reduce(jnp.logical_and, conditions)

    barrier = pltpu.get_barrier_semaphore()
    right_two, left_two = lax.rem(me + 2, n), lax.rem(me + n - 2, n)
    for other in (left, right, left_two, right_two, far_left, far_right):
        pl.semaphore_signal(barrier, inc=1, device_id={"genome": other},
                            device_id_type=pl.DeviceIdType.MESH)

    def remote(src, dst, send, recv, other):
        return pltpu.make_async_remote_copy(
            src_ref=src, dst_ref=dst, send_sem=send, recv_sem=recv,
            device_id={"genome": other}, device_id_type=pl.DeviceIdType.MESH)

    def channel(index, src, dst, landing, other):
        return lambda c: remote(src.at[c], dst.at[c], sent.at[index, c], got.at[landing, c], other)

    map_f = channel(0, map_f_out, map_f_in, 0, right)
    local_f = channel(1, tail_out, tail_in, 1, right)
    group_f = channel(2, carry_f, enter_f, 2, far_right)
    pass_f = channel(3, enter_f, enter_f, 2, left)
    map_b = channel(4, map_b_out, map_b_in, 3, left)
    local_b = channel(5, upper_out, upper_in, 4, left)
    group_b = channel(6, upper_out, enter_b, 5, far_left)
    pass_b = channel(7, enter_b, enter_b, 5, right)
    pass_f_two = channel(8, enter_f, enter_f, 2, left_two)
    pass_b_two = channel(9, enter_b, enter_b, 5, right_two)

    def pass_on_f(c):
        @pl.when(no(even))
        def _():
            pass_f(c).start()

        @pl.when(both(no(even), q >= 2))
        def _():
            pass_f_two(c).start()

    def pass_on_b(c):
        @pl.when(both(even, q + 1 < group))
        def _():
            pass_b(c).start()

        @pl.when(both(even, q + 2 < group))
        def _():
            pass_b_two(c).start()

    def to_right():
        return remote(left_out, left_in, es.at[0], er.at[0], right)

    def to_left():
        return remote(right_out, right_in, es.at[1], er.at[1], left)

    def ahead(side):
        other = (right, left)[side]
        return (remote(pre_base_out.at[side], pre_base_in.at[side], ps.at[side, 0], pr.at[side, 0], other),
                remote(pre_slope_out.at[side], pre_slope_in.at[side], ps.at[side, 1], pr.at[side, 1], other))

    def each(condition, step):
        @pl.when(condition)
        def _():
            def go(c, _):
                step(c)
                return 0
            lax.fori_loop(0, chunks, go, 0)

    def clear(condition, ref):
        @pl.when(condition)
        def _():
            ref[...] = jnp.zeros_like(ref)

    def unit(condition, ref):
        @pl.when(condition)
        def _():
            row = lax.broadcasted_iota(jnp.int32, (half, half), 0)
            col = lax.broadcasted_iota(jnp.int32, (half, half), 1)
            ref[...] = (row == col).astype(F32).reshape(ref.shape)

    fetch[0].wait()
    hi, lo = halves(inverse_ref[...])
    inv_hi[...] = hi
    inv_lo[...] = lo
    fetch[1].wait()
    z_halves = halves(z_ref[...])
    solved = dot3(z_halves, (inv_hi[pl.ds(top, half), :], inv_lo[pl.ds(top, half), :]), NT)
    tail_out[...] = solved.reshape(chunks, rows, half)
    pl.semaphore_wait(barrier, 6)

    each(both(head, start_group, no(tail)), lambda c: local_f(c).start())

    fetch[2].wait()
    projected = dot3((inv_hi[...], inv_lo[...]), halves(couple_ref[...]), NN)
    hi, lo = halves(projected)
    proj_hi[...] = hi
    proj_lo[...] = lo
    chain = -projected[top:, :]
    chain_t = chain.T
    map_f_out[...] = chain_t.reshape(map_f_out.shape)
    map_b_out[...] = chain.reshape(map_b_out.shape)
    forward_w[...] = stacked(halves(chain_t))
    backward_w[...] = stacked(halves(chain))

    def start_head(c):
        map_f(c).start()
        local_f(c).start()
    each(both(head, no(start_group), no(tail)), start_head)
    each(both(tail, no(end_group), no(head)), lambda c: map_b(c).start())

    clear(head, tail_in)
    clear(tail, upper_in)
    clear(start_group, enter_f)
    clear(end_group, enter_b)
    clear(first, left_in)
    clear(last, right_in)
    unit(jnp.logical_or(head, start_group), map_f_in)
    unit(jnp.logical_or(tail, end_group), map_b_in)

    def step(c):
        map_f(c).wait_recv()
        local_f(c).wait_recv()
        moved = dot_stacked(jnp.concatenate([map_f_in[c], tail_in[c]], axis=0), forward_w[...])
        map_f_out[c] = moved[:half // chunks]
        tail_out[c] = tail_out[c] + moved[half // chunks:]

        @pl.when(no(tail))
        def _():
            map_f(c).start()
            local_f(c).start()
    each(both(no(start_group), no(head)), step)

    def step(c):
        local_f(c).wait_recv()
        tail_out[c] = tail_out[c] + dot_stacked(tail_in[c], forward_w[...])

        @pl.when(no(tail))
        def _():
            local_f(c).start()

        @pl.when(both(tail, start_group, no(end_group)))
        def _():
            carry_f[c] = tail_out[c]
            group_f(c).start()
    each(both(start_group, no(head)), step)
    if group == 1:
        def step(c):
            carry_f[c] = tail_out[c]
            group_f(c).start()
        each(both(start_group, no(end_group)), step)

    solved_top = dot3(z_halves, (inv_hi[pl.ds(0, top), :], inv_lo[pl.ds(0, top), :]), NT)
    top_rows[...] = solved_top.reshape(chunks, rows, top)

    def step(c):
        map_b(c).wait_recv()
        map_b_out[c] = dot_stacked(map_b_in[c], backward_w[...])

        @pl.when(no(head))
        def _():
            map_b(c).start()
    each(both(no(end_group), no(tail)), step)

    fetch[3].wait()
    fetch[4].wait()

    def make_mask():
        spread = 128
        units = anchor_ref.shape[1]
        nearest = jnp.broadcast_to(anchor_ref[...], (spread, units)).T
        start = me * typed - half
        lanes = lax.broadcasted_iota(jnp.int32, (units, spread), 1)
        for j in range(0, typed + 2 * half, spread):
            within = jnp.abs(lanes + (start + j) - nearest) <= half
            coef = coef_ref[:, j:j + spread].astype(F32)
            masked[:, j:j + spread] = jnp.where(within, coef, 0.0).astype(BF16)

    @pl.when(g >= count // 2)
    def _():
        make_mask()

    def prepare():
        proj = (proj_hi[...], proj_lo[...])
        proj_top = (proj_hi[pl.ds(0, top), :], proj_lo[pl.ds(0, top), :])
        above = top_rows[...].reshape(traits, top) - dot3(
            halves(tail_in[...].reshape(traits, half)), proj_top, NT)
        top_rows[...] = above.reshape(chunks, rows, top)
        all_rows = jnp.concatenate([above, tail_out[...].reshape(traits, half)], axis=1)
        upper_out[...] = dot3(halves(all_rows), proj, NN).reshape(chunks, rows, half)

        @pl.when(no(start_group))
        def _():
            slope_top = -dot3(halves(map_f_in[...].reshape(half, half)), proj_top, NT)
            slope = jnp.concatenate([slope_top, map_f_out[...].reshape(half, half)], axis=1)
            slope_halves = halves(slope)
            enter_rows_w[...] = stacked(slope_halves)
            enter_add_w[...] = stacked(halves(dot3(slope_halves, proj, NN)))

    relay = both(no(start_group), no(end_group), tail)

    @pl.when(no(relay))
    def _():
        prepare()

    @pl.when(relay)
    def _():
        whole = stacked(halves(map_f_out[...].reshape(half, half)))

        def go(c, _):
            group_f(c).wait_recv()
            pass_on_f(c)
            carry_f[c] = tail_out[c] + dot_stacked(enter_f[c], whole)
            group_f(c).start()
            return 0
        lax.fori_loop(0, chunks, go, 0)
        prepare()

    def step(c):
        group_f(c).wait_recv()
        pass_on_f(c)
    each(both(no(start_group), no(end_group), no(tail)), step)

    @pl.when(both(no(start_group), no(end_group)))
    def _():
        add = dot_stacked(enter_f[...].reshape(traits, half), enter_add_w[...])
        upper_out[...] += add.reshape(chunks, rows, half)

    each(both(tail, no(head), no(end_group)), lambda c: local_b(c).start())

    def step(c):
        local_b(c).wait_recv()
        upper_out[c] = upper_out[c] + dot_stacked(upper_in[c], backward_w[...])

        @pl.when(no(head))
        def _():
            local_b(c).start()
    each(both(no(tail), no(end_group)), step)

    def step(c):
        @pl.when(no(start_group))
        def _():
            group_f(c).wait_recv()
            pass_on_f(c)
            upper_out[c] = upper_out[c] + dot_stacked(enter_f[c], enter_add_w[...])

        @pl.when(no(tail))
        def _():
            local_b(c).wait_recv()
            upper_out[c] = upper_out[c] + dot_stacked(upper_in[c], backward_w[...])

        @pl.when(no(head))
        def _():
            local_b(c).start()

        @pl.when(both(head, no(start_group)))
        def _():
            group_b(c).start()
    each(end_group, step)

    all_rows = jnp.concatenate([top_rows[...].reshape(traits, top),
                                tail_out[...].reshape(traits, half)], axis=1)
    base[...] = all_rows

    @pl.when(no(start_group))
    def _():
        base[...] += dot_stacked(enter_f[...].reshape(traits, half), enter_rows_w[...])

    base[:, top:] -= upper_in[...].reshape(traits, half)
    base[...] = dot3(halves(base[...]), (inv_hi[...], inv_lo[...]), NN)

    @pl.when(no(end_group))
    def _():
        slope = dot3(halves(map_b_in[...].reshape(half, half)),
                     (inv_hi[pl.ds(top, half), :], inv_lo[pl.ds(top, half), :]), NN)
        enter_base_w[...] = stacked(halves(slope))
        pre_base_out[0] = base[:, top:]
        pre_slope_out[0] = slope[:, top:]
        pre_base_out[1] = base[:, :half]
        pre_slope_out[1] = slope[:, :half]
        for copy in ahead(0):
            copy.start()

        @pl.when(no(head))
        def _():
            for copy in ahead(1):
                copy.start()

    @pl.when(g < count // 2)
    def _():
        make_mask()

    def drain_early():
        each(both(no(start_group), no(tail)), lambda c: map_f(c).wait_send())
        each(no(tail), lambda c: local_f(c).wait_send())
        each(both(tail, no(end_group)), lambda c: group_f(c).wait_send())
        each(both(no(even), no(start_group)), lambda c: pass_f(c).wait_send())
        each(both(no(even), q >= 2, no(start_group)), lambda c: pass_f_two(c).wait_send())
        each(both(no(end_group), no(head)), lambda c: map_b(c).wait_send())
        each(no(head), lambda c: local_b(c).wait_send())

    @pl.when(g < count // 2)
    def _():
        drain_early()

    @pl.when(both(no(end_group), head))
    def _():
        whole = stacked(halves(map_b_out[...].reshape(half, half)))

        def go(c, _):
            group_b(c).wait_recv()
            pass_on_b(c)

            @pl.when(no(start_group))
            def _():
                upper_out[c] = upper_out[c] + dot_stacked(enter_b[c], whole)
                group_b(c).start()
            return 0
        lax.fori_loop(0, chunks, go, 0)

    def step(c):
        group_b(c).wait_recv()
        pass_on_b(c)
    each(both(no(end_group), no(head)), step)

    @pl.when(no(end_group))
    def _():
        base[...] -= dot_stacked(enter_b[...].reshape(traits, half), enter_base_w[...])

    weights = base[...].astype(BF16)
    left_out[...] = weights[:, top:]
    right_out[...] = weights[:, :half]

    late_right = both(end_group, no(last))
    late_left = both(no(first), jnp.logical_or(head, end_group))

    @pl.when(late_right)
    def _():
        to_right().start()

    @pl.when(late_left)
    def _():
        to_left().start()

    def edge(side, state):
        for copy in ahead(side):
            copy.wait_recv()
        return (pre_base_in[side] - dot_stacked(
            state.reshape(traits, half), stacked(halves(pre_slope_in[side])))).astype(BF16)

    @pl.when(both(no(end_group), no(head)))
    def _():
        left_in[...] = edge(0, enter_b[...])

    @pl.when(both(head, no(start_group)))
    def _():
        left_in[...] = edge(0, upper_out[...])

    @pl.when(both(no(end_group), no(tail)))
    def _():
        right_in[...] = edge(1, enter_b[...])

    out_ref[...] = product(weights, masked[:, half:half + typed], NT)

    @pl.when(both(no(last), jnp.logical_or(tail, end_group)))
    def _():
        to_left().wait_recv()

    out_ref[...] += product(right_in[...], masked[:, half + typed:], NT)

    @pl.when(both(end_group, no(head)))
    def _():
        to_right().wait_recv()

    out_ref[...] += product(left_in[...], masked[:, :half], NT)

    @pl.when(g >= count // 2)
    def _():
        drain_early()

    each(both(head, no(start_group)), lambda c: group_b(c).wait_send())
    each(both(even, q + 1 < group, no(end_group)), lambda c: pass_b(c).wait_send())
    each(both(even, q + 2 < group, no(end_group)), lambda c: pass_b_two(c).wait_send())

    @pl.when(late_right)
    def _():
        to_right().wait_send()

    @pl.when(late_left)
    def _():
        to_left().wait_send()

    @pl.when(no(end_group))
    def _():
        for copy in ahead(0):
            copy.wait_send()

    @pl.when(both(no(end_group), no(head)))
    def _():
        for copy in ahead(1):
            copy.wait_send()


def per_device(n, z_typed, diag_inverse, coupling, impute_coef, anchor):
    traits, typed = z_typed.shape
    half = coupling.shape[2]
    units, span = impute_coef.shape
    top = typed - half
    chunks = next(k for k in (8, 4, 2, 1) if traits % (16 * k) == half % (8 * k) == 0 or k == 1)
    rows = traits // chunks
    group = 1
    while n % (2 * group) == 0 and 4 * group * group <= n:
        group *= 2
    state = pltpu.VMEM((chunks, rows, half), F32)
    edge = pltpu.VMEM((traits, half), BF16)
    chain_map = pltpu.VMEM((chunks, half // chunks, half), F32)
    return pl.pallas_call(
        functools.partial(kernel, n, group),
        out_shape=jax.ShapeDtypeStruct((traits, units), F32),
        in_specs=[pl.BlockSpec(memory_space=pltpu.HBM)] * 5,
        out_specs=pl.BlockSpec(memory_space=pltpu.VMEM),
        scratch_shapes=[
            pltpu.VMEM((traits, typed), F32), pltpu.VMEM((typed, typed), F32),
            pltpu.VMEM((typed, half), F32), pltpu.VMEM((units, span), BF16),
            pltpu.VMEM((1, units), jnp.int32), pltpu.SemaphoreType.DMA((5,)),
            state, state, state, state, state, state, state,
            chain_map, chain_map, chain_map, chain_map, edge, edge, edge, edge,
            pltpu.VMEM((chunks, rows, top), F32), pltpu.VMEM((traits, typed), F32),
            pltpu.VMEM((3 * half, typed), BF16), pltpu.VMEM((3 * half, half), BF16),
            pltpu.VMEM((3 * half, typed), BF16),
            pltpu.VMEM((3 * half, half), BF16), pltpu.VMEM((3 * half, half), BF16),
            pltpu.VMEM((typed, typed), BF16), pltpu.VMEM((typed, typed), BF16),
            pltpu.VMEM((typed, half), BF16), pltpu.VMEM((typed, half), BF16),
            pltpu.VMEM((units, span), BF16),
            pltpu.VMEM((2, traits, half), F32), pltpu.VMEM((2, traits, half), F32),
            pltpu.VMEM((2, half, half), F32), pltpu.VMEM((2, half, half), F32),
            pltpu.SemaphoreType.DMA((2, 2)), pltpu.SemaphoreType.DMA((2, 2)),
            pltpu.SemaphoreType.DMA((10, chunks)), pltpu.SemaphoreType.DMA((6, chunks)),
            pltpu.SemaphoreType.DMA((2,)), pltpu.SemaphoreType.DMA((2,)),
        ],
        compiler_params=pltpu.CompilerParams(
            collective_id=0, has_side_effects=True, vmem_limit_bytes=63 * 1024 * 1024),
    )(z_typed, diag_inverse[0], coupling[0], impute_coef, anchor.reshape(1, units))


def solution(mesh):
    shared = ("seg", "genome")
    in_specs = (P(None, shared), P(shared, None, None), P(shared, None, None),
                P(shared, None), P(shared))
    return jax.shard_map(
        functools.partial(per_device, mesh.shape["genome"]), mesh=mesh, in_specs=in_specs,
        out_specs=P(None, shared), check_vma=False)
```

```python
import functools

import jax
import jax.numpy as jnp
from jax import lax
from jax.experimental import pallas as pl
from jax.experimental.pallas import tpu as pltpu
from jax.sharding import PartitionSpec as P

F32 = jnp.float32
BF16 = jnp.bfloat16
NN = (((1,), (0,)), ((), ()))
NT = (((1,), (1,)), ((), ()))


def halves(x):
    high = x.astype(BF16)
    return high, (x - high.astype(F32)).astype(BF16)


def product(a, b, dims):
    return lax.dot_general(a, b, dims, preferred_element_type=F32)


def dot3(a, b, dims):
    return product(a[0], b[0], dims) + (product(a[0], b[1], dims) + product(a[1], b[0], dims))


def stacked(b):
    return jnp.concatenate([b[0], b[0], b[1]], axis=0)


def dot_stacked(x, weights):
    high, low = halves(x)
    return product(jnp.concatenate([high, low, high], axis=1), weights, NN)


def kernel(
    n, group, z_hbm, inverse_hbm, couple_hbm, coef_hbm, anchor_hbm, out_ref,
    z_ref, inverse_ref, couple_ref, coef_ref, anchor_ref, fetched,
    tail_in, tail_out, upper_in, upper_out, enter_f, enter_b, carry_f,
    map_f_in, map_f_out, map_b_in, map_b_out, left_in, right_in, left_out, right_out,
    top_rows, base, enter_rows_w, enter_add_w, enter_base_w, forward_w, backward_w, inv_hi, inv_lo, proj_hi, proj_lo, masked,
    pre_base_out, pre_base_in, pre_slope_out, pre_slope_in, ps, pr,
    sent, got, es, er,
):
    me = lax.axis_index("genome")
    count = n // group
    g, q = me // group, lax.rem(me, group)
    first, last = me == 0, me == n - 1
    head, tail = q == 0, q == group - 1
    start_group, end_group = g == 0, g == count - 1
    right, left = lax.rem(me + 1, n), lax.rem(me + n - 1, n)
    far_right, far_left = lax.rem(me + group, n), lax.rem(me + n - group, n)
    chunks, rows, half = tail_in.shape
    typed = inverse_ref.shape[0]
    top = typed - half
    traits = chunks * rows
    no = jnp.logical_not
    even = lax.rem(q, 2) == 0
    fetch = [
        pltpu.make_async_copy(src, dst, fetched.at[i])
        for i, (src, dst) in enumerate((
            (inverse_hbm, inverse_ref), (z_hbm, z_ref), (couple_hbm, couple_ref),
            (anchor_hbm, anchor_ref), (coef_hbm, coef_ref)))]
    for copy in fetch:
        copy.start()

    def both(*conditions):
        return functools.reduce(jnp.logical_and, conditions)

    barrier = pltpu.get_barrier_semaphore()
    right_two, left_two = lax.rem(me + 2, n), lax.rem(me + n - 2, n)
    for other in (left, right, left_two, right_two, far_left, far_right):
        pl.semaphore_signal(barrier, inc=1, device_id={"genome": other},
                            device_id_type=pl.DeviceIdType.MESH)

    def remote(src, dst, send, recv, other):
        return pltpu.make_async_remote_copy(
            src_ref=src, dst_ref=dst, send_sem=send, recv_sem=recv,
            device_id={"genome": other}, device_id_type=pl.DeviceIdType.MESH)

    def channel(index, src, dst, landing, other):
        return lambda c: remote(src.at[c], dst.at[c], sent.at[index, c], got.at[landing, c], other)

    map_f = channel(0, map_f_out, map_f_in, 0, right)
    local_f = channel(1, tail_out, tail_in, 1, right)
    group_f = channel(2, carry_f, enter_f, 2, far_right)
    pass_f = channel(3, enter_f, enter_f, 2, left)
    map_b = channel(4, map_b_out, map_b_in, 3, left)
    local_b = channel(5, upper_out, upper_in, 4, left)
    group_b = channel(6, upper_out, enter_b, 5, far_left)
    pass_b = channel(7, enter_b, enter_b, 5, right)
    pass_f_two = channel(8, enter_f, enter_f, 2, left_two)
    pass_b_two = channel(9, enter_b, enter_b, 5, right_two)

    def pass_on_f(c):
        @pl.when(no(even))
        def _():
            pass_f(c).start()

        @pl.when(both(no(even), q >= 2))
        def _():
            pass_f_two(c).start()

    def pass_on_b(c):
        @pl.when(both(even, q + 1 < group))
        def _():
            pass_b(c).start()

        @pl.when(both(even, q + 2 < group))
        def _():
            pass_b_two(c).start()

    def to_right():
        return remote(left_out, left_in, es.at[0], er.at[0], right)

    def to_left():
        return remote(right_out, right_in, es.at[1], er.at[1], left)

    def ahead(side):
        other = (right, left)[side]
        return (remote(pre_base_out.at[side], pre_base_in.at[side], ps.at[side, 0], pr.at[side, 0], other),
                remote(pre_slope_out.at[side], pre_slope_in.at[side], ps.at[side, 1], pr.at[side, 1], other))

    early_right = both(no(end_group), no(both(tail, g == count - 2)))

    def each(condition, step):
        @pl.when(condition)
        def _():
            def go(c, _):
                step(c)
                return 0
            lax.fori_loop(0, chunks, go, 0)

    def clear(condition, ref):
        @pl.when(condition)
        def _():
            ref[...] = jnp.zeros_like(ref)

    def unit(condition, ref):
        @pl.when(condition)
        def _():
            row = lax.broadcasted_iota(jnp.int32, (half, half), 0)
            col = lax.broadcasted_iota(jnp.int32, (half, half), 1)
            ref[...] = (row == col).astype(F32).reshape(ref.shape)

    fetch[0].wait()
    hi, lo = halves(inverse_ref[...])
    inv_hi[...] = hi
    inv_lo[...] = lo
    fetch[1].wait()
    z_halves = halves(z_ref[...])
    solved = dot3(z_halves, (inv_hi[pl.ds(top, half), :], inv_lo[pl.ds(top, half), :]), NT)
    tail_out[...] = solved.reshape(chunks, rows, half)
    pl.semaphore_wait(barrier, 6)

    each(both(head, start_group, no(tail)), lambda c: local_f(c).start())

    fetch[2].wait()
    projected = dot3((inv_hi[...], inv_lo[...]), halves(couple_ref[...]), NN)
    hi, lo = halves(projected)
    proj_hi[...] = hi
    proj_lo[...] = lo
    chain = -projected[top:, :]
    chain_t = chain.T
    map_f_out[...] = chain_t.reshape(map_f_out.shape)
    map_b_out[...] = chain.reshape(map_b_out.shape)
    forward_w[...] = stacked(halves(chain_t))
    backward_w[...] = stacked(halves(chain))

    def start_head(c):
        map_f(c).start()
        local_f(c).start()
    each(both(head, no(start_group), no(tail)), start_head)
    each(both(tail, no(end_group), no(head)), lambda c: map_b(c).start())

    clear(head, tail_in)
    clear(tail, upper_in)
    clear(start_group, enter_f)
    clear(end_group, enter_b)
    clear(first, left_in)
    clear(last, right_in)
    unit(jnp.logical_or(head, start_group), map_f_in)
    unit(jnp.logical_or(tail, end_group), map_b_in)

    def step(c):
        map_f(c).wait_recv()
        local_f(c).wait_recv()
        moved = dot_stacked(jnp.concatenate([map_f_in[c], tail_in[c]], axis=0), forward_w[...])
        map_f_out[c] = moved[:half // chunks]
        tail_out[c] = tail_out[c] + moved[half // chunks:]

        @pl.when(no(tail))
        def _():
            map_f(c).start()
            local_f(c).start()
    each(both(no(start_group), no(head)), step)

    def step(c):
        local_f(c).wait_recv()
        tail_out[c] = tail_out[c] + dot_stacked(tail_in[c], forward_w[...])

        @pl.when(no(tail))
        def _():
            local_f(c).start()

        @pl.when(both(tail, start_group, no(end_group)))
        def _():
            carry_f[c] = tail_out[c]
            group_f(c).start()
    each(both(start_group, no(head)), step)
    if group == 1:
        def step(c):
            carry_f[c] = tail_out[c]
            group_f(c).start()
        each(both(start_group, no(end_group)), step)

    solved_top = dot3(z_halves, (inv_hi[pl.ds(0, top), :], inv_lo[pl.ds(0, top), :]), NT)
    top_rows[...] = solved_top.reshape(chunks, rows, top)

    def step(c):
        map_b(c).wait_recv()
        map_b_out[c] = dot_stacked(map_b_in[c], backward_w[...])

        @pl.when(no(head))
        def _():
            map_b(c).start()
    each(both(no(end_group), no(tail)), step)

    fetch[3].wait()
    fetch[4].wait()

    def make_mask():
        spread = 128
        units = anchor_ref.shape[1]
        nearest = jnp.broadcast_to(anchor_ref[...], (spread, units)).T
        start = me * typed - half
        lanes = lax.broadcasted_iota(jnp.int32, (units, spread), 1)
        for j in range(0, typed + 2 * half, spread):
            within = jnp.abs(lanes + (start + j) - nearest) <= half
            coef = coef_ref[:, j:j + spread].astype(F32)
            masked[:, j:j + spread] = jnp.where(within, coef, 0.0).astype(BF16)

    @pl.when(g >= count // 2)
    def _():
        make_mask()

    def prepare():
        proj = (proj_hi[...], proj_lo[...])
        proj_top = (proj_hi[pl.ds(0, top), :], proj_lo[pl.ds(0, top), :])
        above = top_rows[...].reshape(traits, top) - dot3(
            halves(tail_in[...].reshape(traits, half)), proj_top, NT)
        top_rows[...] = above.reshape(chunks, rows, top)
        all_rows = jnp.concatenate([above, tail_out[...].reshape(traits, half)], axis=1)
        upper_out[...] = dot3(halves(all_rows), proj, NN).reshape(chunks, rows, half)

        @pl.when(no(start_group))
        def _():
            slope_top = -dot3(halves(map_f_in[...].reshape(half, half)), proj_top, NT)
            slope = jnp.concatenate([slope_top, map_f_out[...].reshape(half, half)], axis=1)
            slope_halves = halves(slope)
            enter_rows_w[...] = stacked(slope_halves)
            enter_add_w[...] = stacked(halves(dot3(slope_halves, proj, NN)))

    relay = both(no(start_group), no(end_group), tail)

    @pl.when(no(relay))
    def _():
        prepare()

    @pl.when(relay)
    def _():
        whole = stacked(halves(map_f_out[...].reshape(half, half)))

        def go(c, _):
            group_f(c).wait_recv()
            pass_on_f(c)
            carry_f[c] = tail_out[c] + dot_stacked(enter_f[c], whole)
            group_f(c).start()
            return 0
        lax.fori_loop(0, chunks, go, 0)
        prepare()

    def step(c):
        group_f(c).wait_recv()
        pass_on_f(c)
    each(both(no(start_group), no(end_group), no(tail)), step)

    @pl.when(both(no(start_group), no(end_group)))
    def _():
        add = dot_stacked(enter_f[...].reshape(traits, half), enter_add_w[...])
        upper_out[...] += add.reshape(chunks, rows, half)

    each(both(tail, no(head), no(end_group)), lambda c: local_b(c).start())

    def step(c):
        local_b(c).wait_recv()
        upper_out[c] = upper_out[c] + dot_stacked(upper_in[c], backward_w[...])

        @pl.when(no(head))
        def _():
            local_b(c).start()
    each(both(no(tail), no(end_group)), step)

    def step(c):
        @pl.when(no(start_group))
        def _():
            group_f(c).wait_recv()
            pass_on_f(c)
            upper_out[c] = upper_out[c] + dot_stacked(enter_f[c], enter_add_w[...])

        @pl.when(no(tail))
        def _():
            local_b(c).wait_recv()
            upper_out[c] = upper_out[c] + dot_stacked(upper_in[c], backward_w[...])

        @pl.when(no(head))
        def _():
            local_b(c).start()

        @pl.when(both(head, no(start_group)))
        def _():
            group_b(c).start()
    each(end_group, step)

    all_rows = jnp.concatenate([top_rows[...].reshape(traits, top),
                                tail_out[...].reshape(traits, half)], axis=1)
    base[...] = all_rows

    @pl.when(no(start_group))
    def _():
        base[...] += dot_stacked(enter_f[...].reshape(traits, half), enter_rows_w[...])

    base[:, top:] -= upper_in[...].reshape(traits, half)
    base[...] = dot3(halves(base[...]), (inv_hi[...], inv_lo[...]), NN)

    @pl.when(no(end_group))
    def _():
        slope = dot3(halves(map_b_in[...].reshape(half, half)),
                     (inv_hi[pl.ds(top, half), :], inv_lo[pl.ds(top, half), :]), NN)
        enter_base_w[...] = stacked(halves(slope))
        pre_base_out[0] = base[:, top:]
        pre_slope_out[0] = slope[:, top:]
        pre_base_out[1] = base[:, :half]
        pre_slope_out[1] = slope[:, :half]
        @pl.when(early_right)
        def _():
            for copy in ahead(0):
                copy.start()

        @pl.when(no(head))
        def _():
            for copy in ahead(1):
                copy.start()

    @pl.when(g < count // 2)
    def _():
        make_mask()

    def drain_early():
        each(both(no(start_group), no(tail)), lambda c: map_f(c).wait_send())
        each(no(tail), lambda c: local_f(c).wait_send())
        each(both(tail, no(end_group)), lambda c: group_f(c).wait_send())
        each(both(no(even), no(start_group)), lambda c: pass_f(c).wait_send())
        each(both(no(even), q >= 2, no(start_group)), lambda c: pass_f_two(c).wait_send())
        each(both(no(end_group), no(head)), lambda c: map_b(c).wait_send())
        each(no(head), lambda c: local_b(c).wait_send())

    @pl.when(g < count // 2)
    def _():
        drain_early()

    @pl.when(both(no(end_group), head))
    def _():
        whole = stacked(halves(map_b_out[...].reshape(half, half)))

        def go(c, _):
            group_b(c).wait_recv()
            pass_on_b(c)

            @pl.when(no(start_group))
            def _():
                upper_out[c] = upper_out[c] + dot_stacked(enter_b[c], whole)
                group_b(c).start()
            return 0
        lax.fori_loop(0, chunks, go, 0)

    def step(c):
        group_b(c).wait_recv()
        pass_on_b(c)
    each(both(no(end_group), no(head)), step)

    @pl.when(no(end_group))
    def _():
        base[...] -= dot_stacked(enter_b[...].reshape(traits, half), enter_base_w[...])

    weights = base[...].astype(BF16)
    left_out[...] = weights[:, top:]
    right_out[...] = weights[:, :half]

    late_right = both(no(last), no(early_right))
    late_left = both(no(first), jnp.logical_or(head, end_group))

    @pl.when(late_right)
    def _():
        to_right().start()

    @pl.when(late_left)
    def _():
        to_left().start()

    def edge(side, state):
        for copy in ahead(side):
            copy.wait_recv()
        return (pre_base_in[side] - dot_stacked(
            state.reshape(traits, half), stacked(halves(pre_slope_in[side])))).astype(BF16)

    @pl.when(both(no(end_group), no(head)))
    def _():
        left_in[...] = edge(0, enter_b[...])

    @pl.when(both(head, no(start_group), no(end_group)))
    def _():
        left_in[...] = edge(0, upper_out[...])

    @pl.when(both(no(end_group), no(tail)))
    def _():
        right_in[...] = edge(1, enter_b[...])

    out_ref[...] = product(weights, masked[:, half:half + typed], NT)

    @pl.when(both(no(last), jnp.logical_or(tail, end_group)))
    def _():
        to_left().wait_recv()

    out_ref[...] += product(right_in[...], masked[:, half + typed:], NT)

    @pl.when(both(end_group, no(first)))
    def _():
        to_right().wait_recv()

    out_ref[...] += product(left_in[...], masked[:, :half], NT)

    @pl.when(g >= count // 2)
    def _():
        drain_early()

    each(both(head, no(start_group)), lambda c: group_b(c).wait_send())
    each(both(even, q + 1 < group, no(end_group)), lambda c: pass_b(c).wait_send())
    each(both(even, q + 2 < group, no(end_group)), lambda c: pass_b_two(c).wait_send())

    @pl.when(late_right)
    def _():
        to_right().wait_send()

    @pl.when(late_left)
    def _():
        to_left().wait_send()

    @pl.when(early_right)
    def _():
        for copy in ahead(0):
            copy.wait_send()

    @pl.when(both(no(end_group), no(head)))
    def _():
        for copy in ahead(1):
            copy.wait_send()


def per_device(n, z_typed, diag_inverse, coupling, impute_coef, anchor):
    traits, typed = z_typed.shape
    half = coupling.shape[2]
    units, span = impute_coef.shape
    top = typed - half
    chunks = next(k for k in (8, 4, 2, 1) if traits % (16 * k) == half % (8 * k) == 0 or k == 1)
    rows = traits // chunks
    group = 1
    while n % (2 * group) == 0 and 4 * group * group <= n:
        group *= 2
    state = pltpu.VMEM((chunks, rows, half), F32)
    edge = pltpu.VMEM((traits, half), BF16)
    chain_map = pltpu.VMEM((chunks, half // chunks, half), F32)
    return pl.pallas_call(
        functools.partial(kernel, n, group),
        out_shape=jax.ShapeDtypeStruct((traits, units), F32),
        in_specs=[pl.BlockSpec(memory_space=pltpu.HBM)] * 5,
        out_specs=pl.BlockSpec(memory_space=pltpu.VMEM),
        scratch_shapes=[
            pltpu.VMEM((traits, typed), F32), pltpu.VMEM((typed, typed), F32),
            pltpu.VMEM((typed, half), F32), pltpu.VMEM((units, span), BF16),
            pltpu.VMEM((1, units), jnp.int32), pltpu.SemaphoreType.DMA((5,)),
            state, state, state, state, state, state, state,
            chain_map, chain_map, chain_map, chain_map, edge, edge, edge, edge,
            pltpu.VMEM((chunks, rows, top), F32), pltpu.VMEM((traits, typed), F32),
            pltpu.VMEM((3 * half, typed), BF16), pltpu.VMEM((3 * half, half), BF16),
            pltpu.VMEM((3 * half, typed), BF16),
            pltpu.VMEM((3 * half, half), BF16), pltpu.VMEM((3 * half, half), BF16),
            pltpu.VMEM((typed, typed), BF16), pltpu.VMEM((typed, typed), BF16),
            pltpu.VMEM((typed, half), BF16), pltpu.VMEM((typed, half), BF16),
            pltpu.VMEM((units, span), BF16),
            pltpu.VMEM((2, traits, half), F32), pltpu.VMEM((2, traits, half), F32),
            pltpu.VMEM((2, half, half), F32), pltpu.VMEM((2, half, half), F32),
            pltpu.SemaphoreType.DMA((2, 2)), pltpu.SemaphoreType.DMA((2, 2)),
            pltpu.SemaphoreType.DMA((10, chunks)), pltpu.SemaphoreType.DMA((6, chunks)),
            pltpu.SemaphoreType.DMA((2,)), pltpu.SemaphoreType.DMA((2,)),
        ],
        compiler_params=pltpu.CompilerParams(
            collective_id=0, has_side_effects=True, vmem_limit_bytes=63 * 1024 * 1024),
    )(z_typed, diag_inverse[0], coupling[0], impute_coef, anchor.reshape(1, units))


def solution(mesh):
    shared = ("seg", "genome")
    in_specs = (P(None, shared), P(shared, None, None), P(shared, None, None),
                P(shared, None), P(shared))
    return jax.shard_map(
        functools.partial(per_device, mesh.shape["genome"]), mesh=mesh, in_specs=in_specs,
        out_specs=P(None, shared), check_vma=False)
```
